32 devices in a mesh: ifg: 8 (over z, core), strip: 4 (over y, x).
Axes of the slice: x: 2, y: 2, z: 4, core: 2. Of those that a mesh axis runs over, the one named last changes fastest.
Arguments:
- grad_x: float32 [64, 256, 1024], P('ifg', 'strip'), may hold values from -3 to 3
- grad_y: float32 [64, 256, 1024], P('ifg', 'strip'), may hold values from -3 to 3
- coherence: float32 [64, 256, 1024], P('ifg', 'strip'), may hold values from 0 to 1, as said below
- pairs: int32 [64, 2], replicated, may hold values from 0 to 31, as said below
Outputs:
- unwrapped: float32 [64, 256, 1024], P('ifg', 'strip')
- series: float32 [32, 256, 1024], P('ifg', 'strip')
The draws below stay inside these ranges and needn't reach their ends.
Inputs may be any that keep to these rules, and one draw needn't show every extreme that they name: Every row names an earlier date first and a later date second; the pairs connect all 32 dates. `coherence`: positive weights.
All inputs are finite; a program needn't handle non-finite values.
Results may differ from the reference program's by a relative error of at most 0.0003.
Values sent between devices are 32-bit elements; how exact they have to be, the bound alone decides.
No kernel may reach another device: no remote copies, remote signals or barrier semaphores. Data moves between devices by JAX's collectives and lax.ppermute only.
A program may use at most 64 MiB of HBM per device.

```python
import jax
import jax.numpy as jnp
from jax import lax

IFGS = 64
DATES = 32
COLS = 1024
ITERS = 3
NROWS = 256


def draw_coherence(key, part):
    first = jax.random.fold_in(key, 0)
    rows = jnp.arange(NROWS, dtype=jnp.float32) / NROWS
    ramp = 0.33 + 0.67 * rows
    base = jax.random.uniform(first, (IFGS, NROWS, COLS), jnp.float32, 0.3, 1.0)
    return (base * ramp[None, :, None]).astype(jnp.float32)


def draw_pairs(key, part):
    key_first, key_span, key_order = jax.random.split(key, 3)
    extra = IFGS - DATES + 1
    chain_first = jnp.arange(DATES - 1, dtype=jnp.int32)
    extra_first = jax.random.randint(key_first, (extra,), 0, DATES - 1).astype(jnp.int32)
    spans = jax.random.randint(key_span, (extra,), 1, 6).astype(jnp.int32)
    extra_second = jnp.minimum(extra_first + spans, DATES - 1)
    earlier = jnp.concatenate([chain_first, extra_first])
    later = jnp.concatenate([chain_first + 1, extra_second])
    order = jax.random.permutation(key_order, IFGS)
    return jnp.stack([earlier, later], axis=1)[order].astype(jnp.int32)


def block_scale(key, dims, cuts, low, top_value):
    level = 1.0
    for dim, blocks in cuts:
        draws = jax.random.uniform(jax.random.fold_in(jax.random.fold_in(key, 6), dim), (blocks,), jnp.float32, low / len(cuts), top_value / len(cuts))
        level = level * jnp.repeat(jnp.exp(draws), dims[dim] // blocks).reshape((-1,) + (1,) * (len(dims) - 1 - dim))
    return level


def setup_inputs(seed: int = 0) -> dict:
    key_list = jax.random.split(jax.random.key(seed), 5)
    return {
        "grad_x": jnp.clip(jax.random.uniform(key_list[0], (IFGS, NROWS, COLS), jnp.float32, -3.0, 3.0) * block_scale(key_list[0], (IFGS, NROWS, COLS), ((0, 8), (1, 4)), -0.4, 0.0), -3.0, 3.0),
        "grad_y": jnp.clip(jax.random.uniform(key_list[1], (IFGS, NROWS, COLS), jnp.float32, -3.0, 3.0) * block_scale(key_list[1], (IFGS, NROWS, COLS), ((0, 8), (1, 4)), -0.4, 0.0), -3.0, 3.0),
        "coherence": draw_coherence(jax.random.fold_in(key_list[4], 71), 0),
        "pairs": draw_pairs(jax.random.fold_in(key_list[4], 71), 0),
    }


damping = 0.1

def prev_col(field):
    return jnp.pad(field, ((0, 0), (0, 0), (1, 0)))[:, :, :-1]

def prev_row(field):
    return jnp.pad(field, ((0, 0), (1, 0), (0, 0)))[:, :-1, :]

def weights_of(coherence):
    wx = jnp.pad(coherence[:, :, :-1] * coherence[:, :, 1:], ((0, 0), (0, 0), (0, 1)))
    wy = jnp.pad(coherence[:, :-1, :] * coherence[:, 1:, :], ((0, 0), (0, 1), (0, 0)))
    return (wx, wy)

def divergence(flux_x, flux_y):
    return flux_x - prev_col(flux_x) + flux_y - prev_row(flux_y)

def operate(field, wx, wy):
    diff_x = jnp.pad(field[:, :, 1:] - field[:, :, :-1], ((0, 0), (0, 0), (0, 1)))
    diff_y = jnp.pad(field[:, 1:, :] - field[:, :-1, :], ((0, 0), (0, 1), (0, 0)))
    return damping * field - divergence(wx * diff_x, wy * diff_y)

def inverse_map(pairs):
    slots = jnp.arange(DATES, dtype=jnp.int32)
    design = (pairs[:, 1:2] == slots[None, :]).astype(jnp.float32) - (pairs[:, 0:1] == slots[None, :]).astype(jnp.float32)
    normal = jnp.dot(design.T, design, precision=lax.Precision.HIGHEST) + 1.0
    factor = jnp.linalg.cholesky(normal)
    return jax.scipy.linalg.cho_solve((factor, True), design.T)

def reference(grad_x, grad_y, coherence, pairs):
    wx, wy = weights_of(coherence)
    rhs = -divergence(wx * grad_x, wy * grad_y)
    solution = jnp.zeros_like(rhs)
    residual = rhs
    direction = rhs
    norm_now = jnp.sum(residual * residual, axis=(1, 2))
    for step in range(ITERS):
        image = operate(direction, wx, wy)
        alpha = norm_now / jnp.sum(direction * image, axis=(1, 2))
        solution = solution + alpha[:, None, None] * direction
        residual = residual - alpha[:, None, None] * image
        norm_next = jnp.sum(residual * residual, axis=(1, 2))
        direction = residual + (norm_next / norm_now)[:, None, None] * direction
        norm_now = norm_next
    mapping = inverse_map(pairs)
    series = jnp.einsum('dk,krc->drc', mapping, solution, precision=lax.Precision.HIGHEST)
    return (solution, series)
```

```python
import jax
import jax.numpy as jnp
from jax import lax
from jax.experimental import pallas as pl
from jax.experimental.pallas import tpu as pltpu
from jax.sharding import PartitionSpec as P

DATES = 32
CHUNKS = 4
damping = 0.1
TINY = 1e-6
F32 = jnp.float32
ANY = pl.BlockSpec(memory_space=pl.ANY)
SMEM = pl.BlockSpec(memory_space=pltpu.SMEM)
VMEM = pl.BlockSpec(memory_space=pltpu.VMEM)


def room(mib):
    return pltpu.CompilerParams(vmem_limit_bytes=mib * 2**20)


def near(x):
    return pltpu.with_memory_space_constraint(x, pltpu.VMEM)


def in_vmem(*shape):
    return pltpu.VMEM(shape, F32)


def next_col(x):
    return pltpu.roll(x, x.shape[1] - 1, axis=1)


def prev_col(x):
    return pltpu.roll(x, 1, axis=1)


def col_weights(c):
    lane = lax.broadcasted_iota(jnp.int32, c.shape, 1)
    return jnp.where(lane < c.shape[1] - 1, c * next_col(c), 0.0)


def col_part(w, f):
    fx = w * (f - next_col(f))
    return fx - prev_col(fx)


def folded(x):
    parts = [x[:, i : i + 128] for i in range(0, x.shape[1], 128)]
    while len(parts) > 1:
        parts = [sum(parts[i : i + 2][1:], parts[i]) for i in range(0, len(parts), 2)]
    return parts[0]


def inverse_map(pairs):
    slots = jnp.arange(DATES, dtype=jnp.int32)
    design = (pairs[:, 1:2] == slots[None, :]).astype(F32) - (
        pairs[:, 0:1] == slots[None, :]
    ).astype(F32)
    normal = jnp.dot(design.T, design, precision=lax.Precision.HIGHEST) + 1.0
    factor = jnp.linalg.cholesky(normal)
    return jax.scipy.linalg.cho_solve((factor, True), design.T)


def edges(coh, gx, gy):
    count, rows, cols = coh.shape
    last_tile = rows // 8 - 1

    def body(ct, xt, yt, cb, xb, yb, down, up):
        row = lax.broadcasted_iota(jnp.int32, (8, cols), 0)

        def partial_rhs(c, x, y):
            fx = col_weights(c) * x
            fy = jnp.where(row < 7, c * pltpu.roll(c, 7, axis=0) * y, 0.0)
            return -(fx - prev_col(fx) + fy - pltpu.roll(fy, 1, axis=0))

        for k in range(count):
            c, y = (cb[k], yb[k])
            r = partial_rhs(c, xb[k], y)
            down[0, k : k + 1, :] = r[6:7]
            down[1, k : k + 1, :] = r[7:8]
            down[2, k : k + 1, :] = y[7:8]
            down[3, k : k + 1, :] = c[6:7]
            down[4, k : k + 1, :] = c[7:8]
            c = ct[k]
            r = partial_rhs(c, xt[k], yt[k])
            for i in range(3):
                up[i, k : k + 1, :] = r[i : i + 1]
                up[3 + i, k : k + 1, :] = c[i : i + 1]

    top = pl.BlockSpec((count, 8, cols), lambda i: (0, 0, 0))
    bottom = pl.BlockSpec((count, 8, cols), lambda i: (0, last_tile, 0))
    return pl.pallas_call(
        body,
        grid=(1,),
        in_specs=[top, top, top, bottom, bottom, bottom],
        out_specs=[
            pl.BlockSpec((5, count, cols), lambda i: (0, 0, 0)),
            pl.BlockSpec((6, count, cols), lambda i: (0, 0, 0)),
        ],
        out_shape=[
            jax.ShapeDtypeStruct((5, count, cols), F32),
            jax.ShapeDtypeStruct((6, count, cols), F32),
        ],
        name="edges",
        compiler_params=room(8),
    )(coh, gx, gy, coh, gx, gy)


def interior(coh, gx, gy):
    count, rows, cols = coh.shape
    tiles, blocks = (rows // 8, cols // 128)

    def body(c_hbm, x_hbm, y_hbm, r, v, u, wx, wy, extra, mom, cs, xs, ys, sems):
        half = rows // 2

        def copies(s):
            return [
                pltpu.make_async_copy(
                    src.at[:, pl.ds(s * half, half), pl.ds(128 * b, 128)],
                    dst.at[b, :, pl.ds(s * half, half), :],
                    sems.at[s, n, b],
                )
                for n, (src, dst) in enumerate(((c_hbm, cs), (x_hbm, xs), (y_hbm, ys)))
                for b in range(blocks)
            ]

        for s in range(2):
            for copy in copies(s):
                copy.start()

        def row_of(ref, i):
            return jnp.concatenate(
                [
                    ref.at[b].reshape(count * rows, 128)[pl.ds(i, count, stride=rows), :]
                    for b in range(blocks)
                ],
                axis=1,
            )

        fy = jnp.zeros((count, cols), F32)
        for copy in copies(0):
            copy.wait()
        c = row_of(cs, 0)
        extra[0] = c
        for at in range(rows):
            if at == half - 1:
                for copy in copies(1):
                    copy.wait()
            w = col_weights(c)
            fx = w * row_of(xs, at)
            rhs = prev_col(fx) - fx + fy
            wx[at] = w
            if at < rows - 1:
                later = row_of(cs, at + 1)
                h = c * later
                wy[at] = h
                fy = h * row_of(ys, at)
                rhs = rhs - fy
                c = later
            else:
                wy[at] = jnp.zeros((count, cols), F32)
                extra[1] = c
                extra[2] = row_of(ys, at)
            r[at] = rhs

        def apply_to(src, dst, first, bound, near_bound):
            def tile(t, carry, low, high):
                fy, a, b = carry
                for i in range(8):
                    at = 8 * t + i
                    f = src[at]
                    after = src[jnp.minimum(at + 1, rows - 1)] if i == 7 else src[at + 1]
                    now = wy[at] * (f - after)
                    g = col_part(wx[at], f) + now - fy
                    fy = now
                    dst[at] = g
                    if low is None or low + i >= bound and high - i >= bound:
                        a = a + folded(f * f)
                    if low is None or low + i >= near_bound and high - i >= near_bound:
                        b = b + folded(f * g)
                return fy, a, b

            none = jnp.zeros((count, 128), F32)
            carry = (jnp.zeros((count, cols), F32), none, none)
            carry = tile(0, carry, 0, rows - 1)
            carry = lax.fori_loop(1, tiles - 1, lambda t, c: tile(t, c, None, None), carry)
            _, a, b = tile(tiles - 1, carry, rows - 8, 7)
            mom[first] = a
            mom[first + 1] = b

        apply_to(r, v, 0, 1, 2)
        apply_to(v, u, 2, 2, 3)

        def energy(t, carry, low, high):
            a, b = carry
            for i in range(8):
                if low is not None and (low + i < 3 or high - i < 3):
                    continue
                at = 8 * t + i
                f = u[at]
                d = f - next_col(f)
                e = wx[at] * d * d
                if low is None or high - i >= 4:
                    d = f - u[at + 1]
                    e = e + wy[at] * d * d
                a = a + folded(f * f)
                b = b + folded(e)
            return a, b

        none = jnp.zeros((count, 128), F32)
        carry = energy(0, (none, none), 0, rows - 1)
        carry = lax.fori_loop(1, tiles - 1, lambda t, c: energy(t, c, None, None), carry)
        mom[4], mom[5] = energy(tiles - 1, carry, rows - 8, 7)

    field = in_vmem(rows, count, cols)
    staged = pltpu.VMEM((blocks, count, rows, 128), F32)
    return pl.pallas_call(
        body,
        in_specs=[ANY] * 3,
        out_specs=[VMEM] * 7,
        out_shape=[field] * 5 + [in_vmem(3, count, cols), in_vmem(6, count, 128)],
        scratch_shapes=[staged] * 3 + [pltpu.SemaphoreType.DMA((2, 3, blocks))],
        name="interior",
        compiler_params=room(12),
    )(coh, gx, gy)


def join(above, below, r, v, u, wx, wy, extra, mom):
    rows, count, cols = r.shape

    def body(ab, be, r_in, v_in, u_in, wx_ref, wy_ref, ex, m_in, r_out, v_out, u_out, out):
        end = rows - 1
        rr, vv, uu = ({}, {}, {})
        gx_w, gy_w = ({}, {})
        for i in (0, 1, 2, 3, end - 3, end - 2, end - 1, end):
            gx_w[i] = wx_ref[i]
            if i != end:
                gy_w[i] = wy_ref[i]
        gx_w[-1] = col_weights(ab[4])
        gy_w[-1] = ab[4] * ex[0]
        gy_w[-2] = ab[3] * ab[4]
        gy_w[end] = ex[1] * be[3]
        gy_w[end + 1] = be[3] * be[4]
        gy_w[end + 2] = be[4] * be[5]
        gx_w[end + 1] = col_weights(be[3])
        gx_w[end + 2] = col_weights(be[4])
        top = gy_w[-1] * ab[2]
        low = gy_w[end] * ex[2]
        rr[-2] = ab[0]
        rr[-1] = ab[1] - top
        rr[0] = r_in[0] + top
        rr[1], rr[2] = (r_in[1], r_in[2])
        rr[end - 2], rr[end - 1] = (r_in[end - 2], r_in[end - 1])
        rr[end] = r_in[end] - low
        rr[end + 1] = be[0] + low
        rr[end + 2] = be[1]
        rr[end + 3] = be[2]
        r_out[0] = rr[0]
        r_out[end] = rr[end]

        def applied(f, i):
            return (
                col_part(gx_w[i], f[i]) + gy_w[i] * (f[i] - f[i + 1]) - gy_w[i - 1] * (f[i - 1] - f[i])
            )

        sums = [m_in[j] for j in range(6)]

        def add(j, x):
            sums[j] = sums[j] + folded(x)

        for i in (-1, 0, 1, end - 1, end, end + 1, end + 2):
            vv[i] = applied(rr, i)
            if 0 <= i <= end:
                v_out[i] = vv[i]
        vv[2], vv[3] = (v_in[2], v_in[3])
        vv[end - 2], vv[end - 3] = (v_in[end - 2], v_in[end - 3])
        for i in (0, 1, 2, end - 2, end - 1, end, end + 1):
            uu[i] = applied(vv, i)
            if i <= end:
                u_out[i] = uu[i]
        uu[3], uu[end - 3] = (u_in[3], u_in[end - 3])
        for i in (0, end):
            add(0, rr[i] * rr[i])
        for i in (0, 1, end - 1, end):
            add(1, rr[i] * vv[i])
            add(2, vv[i] * vv[i])
        for i in (0, 1, 2, end - 2, end - 1, end):
            add(3, vv[i] * uu[i])
            add(4, uu[i] * uu[i])
            d = uu[i] - next_col(uu[i])
            h = uu[i] - uu[i + 1]
            add(5, gx_w[i] * d * d + gy_w[i] * h * h)
        h = uu[end - 3] - uu[end - 2]
        add(5, gy_w[end - 3] * h * h)
        lane = lax.broadcasted_iota(jnp.int32, (count, 128), 1)
        line = jnp.zeros((count, 128), F32)
        for j in range(6):
            line = jnp.where(lane == j, jnp.sum(sums[j], axis=1, keepdims=True), line)
        out[...] = line

    field = in_vmem(rows, count, cols)
    return pl.pallas_call(
        body,
        in_specs=[VMEM] * 9,
        out_specs=[VMEM] * 4,
        out_shape=[field] * 3 + [in_vmem(count, 128)],
        input_output_aliases={2: 0, 3: 1, 4: 2},
        name="join",
        compiler_params=room(4),
    )(*(near(x) for x in (above, below, r, v, u, wx, wy, extra, mom)))


def iterate(place, r, v, u, shares, groups, widths):
    rows, count, cols = r.shape
    high = rows // groups
    number = len(shares)

    def body(place_ref, *refs):
        r_ref, v_ref, u_ref = refs[:3]
        terms = [ref[...] for ref in refs[3 : 3 + number]]
        out, keep, beside, *far = refs[3 + number : -2]
        whole, sem = refs[-2:]
        while len(terms) > 1:
            terms = [sum(terms[i : i + 2][1:], terms[i]) for i in range(0, len(terms), 2)]
        m = terms[0]
        m0, m1, m2, m3, m4, m5 = (m[:, j : j + 1] for j in range(6))
        a00 = damping * m0 + m1
        a01 = damping * m1 + m2
        a02 = damping * m2 + m3
        a12 = damping * m3 + m4
        a22 = damping * m4 + m5

        def over(a, b, good):
            return jnp.where(good, a / jnp.where(good, b, 1.0), 0.0)

        ok0 = a00 > 0.0
        l10 = over(a01, a00, ok0)
        l20 = over(a02, a00, ok0)
        d1 = a02 - l10 * a01
        e12 = a12 - l10 * a02
        ok1 = d1 > TINY * a02
        l21 = over(e12, d1, ok1)
        d2 = a22 - l20 * a02 - l21 * e12
        ok2 = ok1 & (d2 > TINY * a22)
        y1 = m1 - l10 * m0
        y2 = m2 - l20 * m0 - l21 * y1
        c2 = over(y2, d2, ok2)
        c1 = over(y1, d1, ok1) - l21 * c2
        c0 = over(m0, a00, ok0) - l10 * c1 - l20 * c2
        c0, c1, c2 = (jnp.broadcast_to(c, (count, cols)) for c in (c0, c1, c2))
        me = place_ref[1]

        def put(ref, at, pitch, x):
            for b in range(ref.shape[0]):
                ref.at[b].reshape(count * pitch, 128)[pl.ds(at, count, stride=pitch), :] = x[
                    :, 128 * b : 128 * b + 128
                ]

        def rows_for(mask, pieces):
            first = jnp.bitwise_xor(me, mask) * high
            for a in range(high):
                at = first + a
                x = c0 * r_ref[at] + c1 * v_ref[at] + c2 * u_ref[at]
                put(whole, at, rows, x)
                left = 0
                for piece in pieces:
                    wide = 128 * piece.shape[0]
                    put(piece, a, high, x[:, left : left + wide])
                    left += wide

        rows_for(0, [keep])
        rows_for(1, [beside])
        for mask in range(2, groups):
            rows_for(mask, [far[(mask - 2) * len(widths) + i] for i in range(len(widths))])
        copies = [
            pltpu.make_async_copy(whole.at[b], out.at[:, :, pl.ds(128 * b, 128)], sem.at[b])
            for b in range(cols // 128)
        ]
        for copy in copies:
            copy.start()
        for copy in copies:
            copy.wait()

    return pl.pallas_call(
        body,
        in_specs=[SMEM] + [VMEM] * (3 + number),
        out_specs=[ANY] + [VMEM] * (2 + (groups - 2) * len(widths)),
        out_shape=[jax.ShapeDtypeStruct((count, rows, cols), F32)]
        + [in_vmem(cols // 128, count, high, 128)] * 2
        + [in_vmem(wide // 128, count, high, 128) for _ in range(groups - 2) for wide in widths],
        scratch_shapes=[
            pltpu.VMEM((cols // 128, count, rows, 128), F32),
            pltpu.SemaphoreType.DMA((cols // 128,)),
        ],
        name="iterate",
        compiler_params=room(6),
    )(place, *(near(x) for x in (r, v, u, *shares)))


def half_sums(mapping, place, left, fields, start=None):
    groups = len(fields)
    blocks, count, high, _ = fields[-1].shape
    dates = mapping.shape[0] // 2
    share = dates // groups
    spots = [(b, a) for b in range(blocks) for a in range(0, high, 8)]

    def body(place_ref, map_ref, *refs):
        h, me = (place_ref[0], place_ref[1])
        us = refs[:groups]
        columns = [(h * groups + jnp.bitwise_xor(me, m)) * count for m in range(groups)]

        def one(d, acc):
            for m in range(groups):
                base = 0 if us[m].shape[0] == blocks else left // 128
                for k in range(count):
                    w = map_ref[d, columns[m] + k]
                    acc = [x + w * us[m][base + b, k, a : a + 8, :] for (b, a), x in zip(spots, acc)]
            return acc

        def store(out, d, acc):
            for (b, a), x in zip(spots, acc):
                out[b, d, a : a + 8, :] = x

        if start is None:

            def step(d, _):
                store(refs[groups], d, one((1 - h) * dates + d, [jnp.zeros((8, 128), F32)] * len(spots)))
                return 0

            lax.fori_loop(0, dates, step, 0)
        else:
            begun = refs[groups]
            for m, out in enumerate(refs[groups + 1 :]):
                first = jnp.bitwise_xor(me, m) * share

                def step(d, _):
                    acc = [begun[b, first + d, a : a + 8, :] for b, a in spots]
                    store(out, d, one(h * dates + first + d, acc))
                    return 0

                lax.fori_loop(0, share, step, 0)

    args = list(fields) + ([] if start is None else [start])
    out_shape = (
        [in_vmem(blocks, dates, high, 128)]
        if start is None
        else [in_vmem(blocks, share, high, 128)] * groups
    )
    return pl.pallas_call(
        body,
        in_specs=[SMEM, SMEM] + [VMEM] * len(args),
        out_specs=[VMEM] * len(out_shape),
        out_shape=out_shape,
        name="cross_sums" if start is None else "own_sums",
        compiler_params=room(4),
    )(place, mapping, *(near(x) for x in args))


def assemble(place, parts, rows, cols):
    groups = len(parts[0])
    _, dates, high, _ = parts[0][0].shape
    flat = [x for chunk in parts for x in chunk]

    def body(place_ref, *refs):
        me, out = (place_ref[1], refs[-1])
        left = 0
        for i in range(len(parts)):
            blocks = parts[i][0].shape[0]
            for m in range(groups):
                first = pl.multiple_of(jnp.bitwise_xor(me, m) * high, 8)
                for b in range(blocks):
                    at = left + 128 * b
                    out[:, pl.ds(first, high), at : at + 128] = refs[i * groups + m][b]
            left += 128 * blocks

    return pl.pallas_call(
        body,
        in_specs=[SMEM] + [VMEM] * len(flat),
        out_specs=VMEM,
        out_shape=jax.ShapeDtypeStruct((dates, rows, cols), F32),
        name="assemble",
        compiler_params=room(4),
    )(place, *(near(x) for x in flat))


def exchange(x, axis, mask):
    size = lax.axis_size(axis)
    return lax.ppermute(x, axis, [(i, i ^ mask) for i in range(size)])


def summands(x, axis):
    size, bit, terms = (lax.axis_size(axis), 1, [x])
    while bit < size:
        if len(terms) > 1:
            terms = [(terms[0] + terms[1]) + (terms[2] + terms[3])]
        masks = [bit, 2 * bit, 3 * bit] if 4 * bit <= size else [bit]
        terms = terms + [exchange(terms[0], axis, m) for m in masks]
        bit *= len(masks) + 1
    return terms


def on_device(grad_x, grad_y, coherence, pairs):
    strips, size = (lax.axis_size("strip"), lax.axis_size("ifg"))
    count, rows, cols = coherence.shape
    groups = size // 2
    widths = [cols // CHUNKS] * CHUNKS
    index = lax.axis_index("ifg").astype(jnp.int32)
    place = jnp.stack([index // groups, index % groups])
    down, up = edges(coherence, grad_x, grad_y)
    forward = [(i, i + 1) for i in range(strips - 1)]
    above = lax.ppermute(down, "strip", forward)
    below = lax.ppermute(up, "strip", [(j, i) for i, j in forward])
    fields = interior(coherence, grad_x, grad_y)
    r, v, u, moments = join(above, below, *fields)
    shares = summands(moments, "strip")
    phase, keep, beside, *far = iterate(place, r, v, u, shares, groups, widths)

    mapping = inverse_map(pairs)
    beside = exchange(beside, "ifg", 1)
    got = [
        [exchange(far[(m - 2) * CHUNKS + i], "ifg", m) for m in range(2, groups)]
        for i in range(CHUNKS)
    ]
    parts, left = ([], 0)
    for i, wide in enumerate(widths):
        mine = [keep, beside] + got[i]
        (other,) = half_sums(mapping, place, left, mine)
        other = exchange(other, "ifg", groups)
        full = half_sums(mapping, place, left, mine, other)
        parts.append([full[0]] + [exchange(full[m], "ifg", m) for m in range(1, groups)])
        left += wide
    return (phase, assemble(place, parts, rows, cols))


def solution(mesh):
    in_specs = (P("ifg", "strip", None), P("ifg", "strip", None), P("ifg", "strip", None), P())
    out_specs = (P("ifg", "strip", None), P("ifg", "strip", None))
    return jax.shard_map(
        on_device, mesh=mesh, in_specs=in_specs, out_specs=out_specs, check_vma=False
    )
```

```python
import jax
import jax.numpy as jnp
from jax import lax
from jax.experimental import pallas as pl
from jax.experimental.pallas import tpu as pltpu
from jax.sharding import PartitionSpec as P

DATES = 32
CHUNKS = 4
PAD = 8
damping = 0.1
TINY = 1e-6
F32 = jnp.float32
ANY = pl.BlockSpec(memory_space=pl.ANY)
SMEM = pl.BlockSpec(memory_space=pltpu.SMEM)
VMEM = pl.BlockSpec(memory_space=pltpu.VMEM)


def room(mib):
    return pltpu.CompilerParams(vmem_limit_bytes=mib * 2**20)


def near(x):
    return pltpu.with_memory_space_constraint(x, pltpu.VMEM)


def far_off(x):
    return pltpu.with_memory_space_constraint(x, pltpu.HBM)


def half_and_member(groups):
    index = lax.axis_index("ifg").astype(jnp.int32)
    return (index // groups, index % groups)


def in_vmem(*shape):
    return pltpu.VMEM(shape, F32)


def next_col(x):
    return pltpu.roll(x, x.shape[1] - 1, axis=1)


def prev_col(x):
    return pltpu.roll(x, 1, axis=1)


def col_weights(c):
    lane = lax.broadcasted_iota(jnp.int32, c.shape, 1)
    return jnp.where(lane < c.shape[1] - 1, c * next_col(c), 0.0)


def col_part(w, f):
    fx = w * (f - next_col(f))
    return fx - prev_col(fx)


def folded(x):
    parts = [x[:, i : i + 128] for i in range(0, x.shape[1], 128)]
    while len(parts) > 1:
        parts = [sum(parts[i : i + 2][1:], parts[i]) for i in range(0, len(parts), 2)]
    return parts[0]


def inverse_map(pairs):
    number = pairs.shape[0]
    wide = -(-(DATES + number) // 128) * 128

    def body(pair, out, work):
        p = pair[...]
        slots = lax.broadcasted_iota(jnp.int32, (DATES, number), 0)
        back = (p[1:2] == slots).astype(F32) - (p[0:1] == slots).astype(F32)
        normal = 1.0 + lax.dot_general(
            back, back, (((1,), (1,)), ((), ())), precision=lax.Precision.HIGHEST, preferred_element_type=F32
        )
        work[...] = jnp.zeros_like(work)
        work[:, :DATES] = normal
        work[:, DATES : DATES + number] = back
        w = work[...]
        row = lax.broadcasted_iota(jnp.int32, (DATES, wide), 0)
        for j in range(DATES):
            pivot = w[j : j + 1] / w[j : j + 1, j : j + 1]
            w = jnp.where(row == j, pivot, w - w[:, j : j + 1] * pivot)
        work[...] = w
        out[...] = work[:, DATES : DATES + number]

    return pl.pallas_call(
        body,
        in_specs=[VMEM],
        out_specs=VMEM,
        out_shape=jax.ShapeDtypeStruct((DATES, number), F32),
        scratch_shapes=[pltpu.VMEM((DATES, wide), F32)],
        name="inverse_map",
        compiler_params=room(2),
    )(pairs.T)


def edges(coh, gx, gy):
    count, rows, cols = coh.shape
    last_tile = rows // 8 - 1

    def body(ct, xt, yt, cb, xb, yb, down, up):
        row = lax.broadcasted_iota(jnp.int32, (8, cols), 0)

        def partial_rhs(c, x, y):
            fx = col_weights(c) * x
            fy = jnp.where(row < 7, c * pltpu.roll(c, 7, axis=0) * y, 0.0)
            return -(fx - prev_col(fx) + fy - pltpu.roll(fy, 1, axis=0))

        for k in range(count):
            c, y = (cb[k], yb[k])
            r = partial_rhs(c, xb[k], y)
            down[0, k : k + 1, :] = r[6:7]
            down[1, k : k + 1, :] = r[7:8]
            down[2, k : k + 1, :] = y[7:8]
            down[3, k : k + 1, :] = c[6:7]
            down[4, k : k + 1, :] = c[7:8]
            c = ct[k]
            r = partial_rhs(c, xt[k], yt[k])
            for i in range(3):
                up[i, k : k + 1, :] = r[i : i + 1]
                up[3 + i, k : k + 1, :] = c[i : i + 1]

    top = pl.BlockSpec((count, 8, cols), lambda i: (0, 0, 0))
    bottom = pl.BlockSpec((count, 8, cols), lambda i: (0, last_tile, 0))
    return pl.pallas_call(
        body,
        grid=(1,),
        in_specs=[top, top, top, bottom, bottom, bottom],
        out_specs=[
            pl.BlockSpec((5, count, cols), lambda i: (0, 0, 0)),
            pl.BlockSpec((6, count, cols), lambda i: (0, 0, 0)),
        ],
        out_shape=[
            jax.ShapeDtypeStruct((5, count, cols), F32),
            jax.ShapeDtypeStruct((6, count, cols), F32),
        ],
        name="edges",
        compiler_params=room(8),
    )(*(far_off(x) for x in (coh, gx, gy, coh, gx, gy)))


def interior(coh, gx, gy):
    count, rows, cols = coh.shape
    tiles, blocks = (rows // 8, cols // 128)

    def body(c_hbm, x_hbm, y_hbm, r, v, u, wx, wy, extra, mom, cs, xs, ys, sems):
        half = rows // 2

        def copies(s):
            return [
                pltpu.make_async_copy(
                    src.at[:, pl.ds(s * half, half), pl.ds(128 * b, 128)],
                    dst.at[b, :, pl.ds(s * half, half), :],
                    sems.at[s, n, b],
                )
                for n, (src, dst) in enumerate(((c_hbm, cs), (x_hbm, xs), (y_hbm, ys)))
                for b in range(blocks)
            ]

        for s in range(2):
            for copy in copies(s):
                copy.start()

        def row_of(ref, i):
            return jnp.concatenate(
                [
                    ref.at[b].reshape(count * (rows + PAD), 128)[pl.ds(i, count, stride=rows + PAD), :]
                    for b in range(blocks)
                ],
                axis=1,
            )

        fy = jnp.zeros((count, cols), F32)
        for copy in copies(0):
            copy.wait()
        c = row_of(cs, 0)
        extra[0] = c
        for at in range(rows):
            if at == half - 1:
                for copy in copies(1):
                    copy.wait()
            w = col_weights(c)
            fx = w * row_of(xs, at)
            rhs = prev_col(fx) - fx + fy
            wx[at] = w
            if at < rows - 1:
                later = row_of(cs, at + 1)
                h = c * later
                wy[at] = h
                fy = h * row_of(ys, at)
                rhs = rhs - fy
                c = later
            else:
                wy[at] = jnp.zeros((count, cols), F32)
                extra[1] = c
                extra[2] = row_of(ys, at)
            r[at] = rhs

        def apply_to(src, dst, first, bound, near_bound):
            def tile(t, carry, low, high):
                fy, a, b = carry
                for i in range(8):
                    at = 8 * t + i
                    f = src[at]
                    after = src[jnp.minimum(at + 1, rows - 1)] if i == 7 else src[at + 1]
                    now = wy[at] * (f - after)
                    g = col_part(wx[at], f) + now - fy
                    fy = now
                    dst[at] = g
                    if low is None or low + i >= bound and high - i >= bound:
                        a = a + folded(f * f)
                    if low is None or low + i >= near_bound and high - i >= near_bound:
                        b = b + folded(f * g)
                return fy, a, b

            none = jnp.zeros((count, 128), F32)
            carry = (jnp.zeros((count, cols), F32), none, none)
            carry = tile(0, carry, 0, rows - 1)
            carry = lax.fori_loop(1, tiles - 1, lambda t, c: tile(t, c, None, None), carry)
            _, a, b = tile(tiles - 1, carry, rows - 8, 7)
            mom[first] = a
            mom[first + 1] = b

        apply_to(r, v, 0, 1, 2)
        apply_to(v, u, 2, 2, 3)

        def energy(t, carry, low, high):
            a, b = carry
            for i in range(8):
                if low is not None and (low + i < 3 or high - i < 3):
                    continue
                at = 8 * t + i
                f = u[at]
                d = f - next_col(f)
                e = wx[at] * d * d
                if low is None or high - i >= 4:
                    d = f - u[at + 1]
                    e = e + wy[at] * d * d
                a = a + folded(f * f)
                b = b + folded(e)
            return a, b

        none = jnp.zeros((count, 128), F32)
        carry = energy(0, (none, none), 0, rows - 1)
        carry = lax.fori_loop(1, tiles - 1, lambda t, c: energy(t, c, None, None), carry)
        mom[4], mom[5] = energy(tiles - 1, carry, rows - 8, 7)

    field = in_vmem(rows, count, cols)
    staged = pltpu.VMEM((blocks, count, rows + PAD, 128), F32)
    return pl.pallas_call(
        body,
        in_specs=[ANY] * 3,
        out_specs=[VMEM] * 7,
        out_shape=[field] * 5 + [in_vmem(3, count, cols), in_vmem(6, count, 128)],
        scratch_shapes=[staged] * 3 + [pltpu.SemaphoreType.DMA((2, 3, blocks))],
        name="interior",
        compiler_params=room(12),
    )(*(far_off(x) for x in (coh, gx, gy)))


def join(above, below, r, v, u, wx, wy, extra, mom):
    rows, count, cols = r.shape

    def body(ab, be, r_in, v_in, u_in, wx_ref, wy_ref, ex, m_in, r_out, v_out, u_out, out):
        end = rows - 1
        rr, vv, uu = ({}, {}, {})
        gx_w, gy_w = ({}, {})
        for i in (0, 1, 2, 3, end - 3, end - 2, end - 1, end):
            gx_w[i] = wx_ref[i]
            if i != end:
                gy_w[i] = wy_ref[i]
        gx_w[-1] = col_weights(ab[4])
        gy_w[-1] = ab[4] * ex[0]
        gy_w[-2] = ab[3] * ab[4]
        gy_w[end] = ex[1] * be[3]
        gy_w[end + 1] = be[3] * be[4]
        gy_w[end + 2] = be[4] * be[5]
        gx_w[end + 1] = col_weights(be[3])
        gx_w[end + 2] = col_weights(be[4])
        top = gy_w[-1] * ab[2]
        low = gy_w[end] * ex[2]
        rr[-2] = ab[0]
        rr[-1] = ab[1] - top
        rr[0] = r_in[0] + top
        rr[1], rr[2] = (r_in[1], r_in[2])
        rr[end - 2], rr[end - 1] = (r_in[end - 2], r_in[end - 1])
        rr[end] = r_in[end] - low
        rr[end + 1] = be[0] + low
        rr[end + 2] = be[1]
        rr[end + 3] = be[2]
        r_out[0] = rr[0]
        r_out[end] = rr[end]

        def applied(f, i):
            return (
                col_part(gx_w[i], f[i]) + gy_w[i] * (f[i] - f[i + 1]) - gy_w[i - 1] * (f[i - 1] - f[i])
            )

        sums = [m_in[j] for j in range(6)]

        def add(j, x):
            sums[j] = sums[j] + folded(x)

        for i in (-1, 0, 1, end - 1, end, end + 1, end + 2):
            vv[i] = applied(rr, i)
            if 0 <= i <= end:
                v_out[i] = vv[i]
        vv[2], vv[3] = (v_in[2], v_in[3])
        vv[end - 2], vv[end - 3] = (v_in[end - 2], v_in[end - 3])
        for i in (0, 1, 2, end - 2, end - 1, end, end + 1):
            uu[i] = applied(vv, i)
            if i <= end:
                u_out[i] = uu[i]
        uu[3], uu[end - 3] = (u_in[3], u_in[end - 3])
        for i in (0, end):
            add(0, rr[i] * rr[i])
        for i in (0, 1, end - 1, end):
            add(1, rr[i] * vv[i])
            add(2, vv[i] * vv[i])
        for i in (0, 1, 2, end - 2, end - 1, end):
            add(3, vv[i] * uu[i])
            add(4, uu[i] * uu[i])
            d = uu[i] - next_col(uu[i])
            h = uu[i] - uu[i + 1]
            add(5, gx_w[i] * d * d + gy_w[i] * h * h)
        h = uu[end - 3] - uu[end - 2]
        add(5, gy_w[end - 3] * h * h)
        lane = lax.broadcasted_iota(jnp.int32, (count, 128), 1)
        line = jnp.zeros((count, 128), F32)
        for j in range(6):
            line = jnp.where(lane == j, jnp.sum(sums[j], axis=1, keepdims=True), line)
        out[...] = line

    field = in_vmem(rows, count, cols)
    return pl.pallas_call(
        body,
        in_specs=[VMEM] * 9,
        out_specs=[VMEM] * 4,
        out_shape=[field] * 3 + [in_vmem(count, 128)],
        input_output_aliases={2: 0, 3: 1, 4: 2},
        name="join",
        compiler_params=room(4),
    )(near(above), near(below), r, v, u, wx, wy, extra, mom)


def iterate(r, v, u, shares, groups, widths):
    rows, count, cols = r.shape
    high = rows // groups
    number = len(shares)

    def body(*refs):
        r_ref, v_ref, u_ref = refs[:3]
        terms = [ref[...] for ref in refs[3 : 3 + number]]
        out, keep, beside, *far = refs[3 + number : -2]
        whole, sem = refs[-2:]
        while len(terms) > 1:
            terms = [sum(terms[i : i + 2][1:], terms[i]) for i in range(0, len(terms), 2)]
        m = terms[0]
        m0, m1, m2, m3, m4, m5 = (m[:, j : j + 1] for j in range(6))
        a00 = damping * m0 + m1
        a01 = damping * m1 + m2
        a02 = damping * m2 + m3
        a12 = damping * m3 + m4
        a22 = damping * m4 + m5

        def over(a, b, good):
            return jnp.where(good, a / jnp.where(good, b, 1.0), 0.0)

        ok0 = a00 > 0.0
        l10 = over(a01, a00, ok0)
        l20 = over(a02, a00, ok0)
        d1 = a02 - l10 * a01
        e12 = a12 - l10 * a02
        ok1 = d1 > TINY * a02
        l21 = over(e12, d1, ok1)
        d2 = a22 - l20 * a02 - l21 * e12
        ok2 = ok1 & (d2 > TINY * a22)
        y1 = m1 - l10 * m0
        y2 = m2 - l20 * m0 - l21 * y1
        c2 = over(y2, d2, ok2)
        c1 = over(y1, d1, ok1) - l21 * c2
        c0 = over(m0, a00, ok0) - l10 * c1 - l20 * c2
        c0, c1, c2 = (jnp.broadcast_to(c, (count, cols)) for c in (c0, c1, c2))
        _, me = half_and_member(groups)

        def put(ref, at, pitch, x):
            for b in range(ref.shape[0]):
                ref.at[b].reshape(count * pitch, 128)[pl.ds(at, count, stride=pitch), :] = x[
                    :, 128 * b : 128 * b + 128
                ]

        def rows_for(mask, pieces):
            first = jnp.bitwise_xor(me, mask) * high
            for a in range(high):
                at = first + a
                x = c0 * r_ref[at] + c1 * v_ref[at] + c2 * u_ref[at]
                put(whole, at, rows + PAD, x)
                left = 0
                for piece in pieces:
                    wide = 128 * piece.shape[0]
                    put(piece, a, high, x[:, left : left + wide])
                    left += wide

        rows_for(0, [keep])
        rows_for(1, [beside])
        for mask in range(2, groups):
            rows_for(mask, [far[(mask - 2) * len(widths) + i] for i in range(len(widths))])
        copies = [
            pltpu.make_async_copy(
                whole.at[b, :, pl.ds(0, rows), :], out.at[:, :, pl.ds(128 * b, 128)], sem.at[b]
            )
            for b in range(cols // 128)
        ]
        for copy in copies:
            copy.start()
        for copy in copies:
            copy.wait()

    return pl.pallas_call(
        body,
        in_specs=[VMEM] * (3 + number),
        out_specs=[ANY] + [VMEM] * (2 + (groups - 2) * len(widths)),
        out_shape=[jax.ShapeDtypeStruct((count, rows, cols), F32)]
        + [in_vmem(cols // 128, count, high, 128)] * 2
        + [in_vmem(wide // 128, count, high, 128) for _ in range(groups - 2) for wide in widths],
        scratch_shapes=[
            pltpu.VMEM((cols // 128, count, rows + PAD, 128), F32),
            pltpu.SemaphoreType.DMA((cols // 128,)),
        ],
        name="iterate",
        compiler_params=room(6),
    )(r, v, u, *(near(x) for x in shares))


def half_sums(mapping, left, fields, start=None):
    groups = len(fields)
    blocks, count, high, _ = fields[-1].shape
    dates = mapping.shape[0] // 2
    share = dates // groups
    spots = [(b, a) for b in range(blocks) for a in range(0, high, 8)]

    def body(map_ref, *refs):
        h, me = half_and_member(groups)
        us = refs[:groups]
        columns = [(h * groups + jnp.bitwise_xor(me, m)) * count for m in range(groups)]

        def one(d, acc):
            for m in range(groups):
                base = 0 if us[m].shape[0] == blocks else left // 128
                for k in range(count):
                    w = map_ref[d, columns[m] + k]
                    acc = [x + w * us[m][base + b, k, a : a + 8, :] for (b, a), x in zip(spots, acc)]
            return acc

        def store(out, d, acc):
            for (b, a), x in zip(spots, acc):
                out[b, d, a : a + 8, :] = x

        if start is None:

            def step(d, _):
                store(refs[groups], d, one((1 - h) * dates + d, [jnp.zeros((8, 128), F32)] * len(spots)))
                return 0

            lax.fori_loop(0, dates, step, 0)
        else:
            begun = refs[groups]
            for m, out in enumerate(refs[groups + 1 :]):
                first = jnp.bitwise_xor(me, m) * share

                def step(d, _):
                    acc = [begun[b, first + d, a : a + 8, :] for b, a in spots]
                    store(out, d, one(h * dates + first + d, acc))
                    return 0

                lax.fori_loop(0, share, step, 0)

    args = list(fields) + ([] if start is None else [start])
    out_shape = (
        [in_vmem(blocks, dates, high, 128)]
        if start is None
        else [in_vmem(blocks, share, high, 128)] * groups
    )
    return pl.pallas_call(
        body,
        in_specs=[SMEM] + [VMEM] * len(args),
        out_specs=[VMEM] * len(out_shape),
        out_shape=out_shape,
        name="cross_sums" if start is None else "own_sums",
        compiler_params=room(4),
    )(mapping, *(near(x) for x in args))


def assemble(parts, rows, cols):
    groups = len(parts[0])
    _, dates, high, _ = parts[0][0].shape
    flat = [x for chunk in parts for x in chunk]

    def body(*refs):
        _, me = half_and_member(groups)
        out = refs[-1]
        left = 0
        for i in range(len(parts)):
            blocks = parts[i][0].shape[0]
            for m in range(groups):
                first = pl.multiple_of(jnp.bitwise_xor(me, m) * high, 8)
                for b in range(blocks):
                    at = left + 128 * b
                    out[:, pl.ds(first, high), at : at + 128] = refs[i * groups + m][b]
            left += 128 * blocks

    return pl.pallas_call(
        body,
        in_specs=[VMEM] * len(flat),
        out_specs=VMEM,
        out_shape=jax.ShapeDtypeStruct((dates, rows, cols), F32),
        name="assemble",
        compiler_params=room(4),
    )(*(near(x) for x in flat))


def exchange(x, axis, mask):
    size = lax.axis_size(axis)
    return lax.ppermute(x, axis, [(i, i ^ mask) for i in range(size)])


def summands(x, axis):
    size, bit, terms = (lax.axis_size(axis), 1, [x])
    while bit < size:
        if len(terms) > 1:
            terms = [(terms[0] + terms[1]) + (terms[2] + terms[3])]
        masks = [bit, 2 * bit, 3 * bit] if 4 * bit <= size else [bit]
        terms = terms + [exchange(terms[0], axis, m) for m in masks]
        bit *= len(masks) + 1
    return terms


def on_device(grad_x, grad_y, coherence, pairs):
    strips, size = (lax.axis_size("strip"), lax.axis_size("ifg"))
    count, rows, cols = coherence.shape
    groups = size // 2
    widths = [cols // CHUNKS] * CHUNKS
    down, up = edges(coherence, grad_x, grad_y)
    forward = [(i, i + 1) for i in range(strips - 1)]
    above = lax.ppermute(down, "strip", forward)
    below = lax.ppermute(up, "strip", [(j, i) for i, j in forward])
    fields = interior(coherence, grad_x, grad_y)
    r, v, u, moments = join(above, below, *fields)
    shares = summands(moments, "strip")
    phase, keep, beside, *far = iterate(r, v, u, shares, groups, widths)

    mapping = inverse_map(pairs)
    beside = exchange(beside, "ifg", 1)
    got = [
        [exchange(far[(m - 2) * CHUNKS + i], "ifg", m) for m in range(2, groups)]
        for i in range(CHUNKS)
    ]
    parts, left = ([], 0)
    for i, wide in enumerate(widths):
        mine = [keep, beside] + got[i]
        (other,) = half_sums(mapping, left, mine)
        other = exchange(other, "ifg", groups)
        full = half_sums(mapping, left, mine, other)
        parts.append([full[0]] + [exchange(full[m], "ifg", m) for m in range(1, groups)])
        left += wide
    return (phase, assemble(parts, rows, cols))


def solution(mesh):
    in_specs = (P("ifg", "strip", None), P("ifg", "strip", None), P("ifg", "strip", None), P())
    out_specs = (P("ifg", "strip", None), P("ifg", "strip", None))
    return jax.shard_map(
        on_device, mesh=mesh, in_specs=in_specs, out_specs=out_specs, check_vma=False
    )
```

```python
import jax
import jax.numpy as jnp
from jax import lax
from jax.experimental import pallas as pl
from jax.experimental.pallas import tpu as pltpu
from jax.sharding import PartitionSpec as P

DATES = 32
SLICES = (1, 2, 2, 2, 1)
CHUNKS = len(SLICES)
PAD = 8
damping = 0.1
TINY = 1e-6
F32 = jnp.float32
ANY = pl.BlockSpec(memory_space=pl.ANY)
SMEM = pl.BlockSpec(memory_space=pltpu.SMEM)
VMEM = pl.BlockSpec(memory_space=pltpu.VMEM)


def room(mib):
    return pltpu.CompilerParams(vmem_limit_bytes=mib * 2**20)


def near(x):
    return pltpu.with_memory_space_constraint(x, pltpu.VMEM)


def far_off(x):
    return pltpu.with_memory_space_constraint(x, pltpu.HBM)


def half_and_member(groups):
    index = lax.axis_index("ifg").astype(jnp.int32)
    return (index // groups, index % groups)


def in_vmem(*shape):
    return pltpu.VMEM(shape, F32)


def turned_cols(x, by, at):
    lane = lax.broadcasted_iota(jnp.int32, (x.shape[0], 128), 1)
    turned = [pltpu.roll(x[:, i : i + 128], by % 128, axis=1) for i in range(0, x.shape[1], 128)]
    moved = turned[-by:] + turned[:-by]
    return jnp.concatenate([jnp.where(lane == at, m, t) for m, t in zip(moved, turned)], axis=1)


def next_col(x):
    return turned_cols(x, -1, 127)


def prev_col(x):
    return turned_cols(x, 1, 0)


def col_weights(c):
    lane = lax.broadcasted_iota(jnp.int32, c.shape, 1)
    return jnp.where(lane < c.shape[1] - 1, c * next_col(c), 0.0)


def col_part(w, f):
    fx = w * (f - next_col(f))
    return fx - prev_col(fx)


def folded(x):
    parts = [x[:, i : i + 128] for i in range(0, x.shape[1], 128)]
    while len(parts) > 1:
        parts = [sum(parts[i : i + 2][1:], parts[i]) for i in range(0, len(parts), 2)]
    return parts[0]


def inverse_map(pairs, groups):
    number = pairs.shape[0]
    inner = number // 2
    wide = -(-(DATES + number) // 128) * 128
    share = DATES // (2 * groups)
    count = number // (2 * groups)

    def body(pair, out, work):
        h, me = half_and_member(groups)

        def twin(i, each):
            return jnp.bitwise_xor(i // each, me) * each + i % each

        d = lax.broadcasted_iota(jnp.int32, (DATES, number), 0)
        half = DATES // 2
        slots = jnp.where(d < half, (1 - h) * half + d, h * half + twin(d % half, share))
        k = lax.broadcasted_iota(jnp.int32, (number, number), 1)
        source = jnp.where(k < inner, h * inner + twin(k % inner, count), (1 - h) * inner + k % inner)
        turn = (source == lax.broadcasted_iota(jnp.int32, (number, number), 0)).astype(F32)
        p = jnp.dot(
            pair[...].astype(F32), turn, precision=lax.Precision.HIGHEST, preferred_element_type=F32
        )
        slots = slots.astype(F32)
        back = (p[1:2] == slots).astype(F32) - (p[0:1] == slots).astype(F32)
        normal = 1.0 + lax.dot_general(
            back, back, (((1,), (1,)), ((), ())), precision=lax.Precision.HIGHEST, preferred_element_type=F32
        )
        work[...] = jnp.zeros_like(work)
        work[:, :DATES] = normal
        work[:, DATES : DATES + number] = back
        w = work[...]
        row = lax.broadcasted_iota(jnp.int32, (DATES, wide), 0)
        for j in range(DATES):
            pivot = w[j : j + 1] / w[j : j + 1, j : j + 1]
            w = jnp.where(row == j, pivot, w - w[:, j : j + 1] * pivot)
        work[...] = w
        out[...] = work[:, DATES : DATES + inner]

    return pl.pallas_call(
        body,
        in_specs=[VMEM],
        out_specs=VMEM,
        out_shape=jax.ShapeDtypeStruct((DATES, inner), F32),
        scratch_shapes=[pltpu.VMEM((DATES, wide), F32)],
        name="inverse_map",
        compiler_params=room(2),
    )(pairs.T)


def edges(coh, gx, gy):
    count, rows, cols = coh.shape
    last_tile = rows // 8 - 1

    def body(ct, xt, yt, cb, xb, yb, down, up):
        row = lax.broadcasted_iota(jnp.int32, (8, cols), 0)

        def partial_rhs(c, x, y):
            fx = col_weights(c) * x
            fy = jnp.where(row < 7, c * pltpu.roll(c, 7, axis=0) * y, 0.0)
            return -(fx - prev_col(fx) + fy - pltpu.roll(fy, 1, axis=0))

        for k in range(count):
            c, y = (cb[k], yb[k])
            r = partial_rhs(c, xb[k], y)
            down[0, k : k + 1, :] = r[6:7]
            down[1, k : k + 1, :] = r[7:8]
            down[2, k : k + 1, :] = y[7:8]
            down[3, k : k + 1, :] = c[6:7]
            down[4, k : k + 1, :] = c[7:8]
            c = ct[k]
            r = partial_rhs(c, xt[k], yt[k])
            for i in range(3):
                up[i, k : k + 1, :] = r[i : i + 1]
                up[3 + i, k : k + 1, :] = c[i : i + 1]

    top = pl.BlockSpec((count, 8, cols), lambda i: (0, 0, 0))
    bottom = pl.BlockSpec((count, 8, cols), lambda i: (0, last_tile, 0))
    return pl.pallas_call(
        body,
        grid=(1,),
        in_specs=[top, top, top, bottom, bottom, bottom],
        out_specs=[
            pl.BlockSpec((5, count, cols), lambda i: (0, 0, 0)),
            pl.BlockSpec((6, count, cols), lambda i: (0, 0, 0)),
        ],
        out_shape=[
            jax.ShapeDtypeStruct((5, count, cols), F32),
            jax.ShapeDtypeStruct((6, count, cols), F32),
        ],
        name="edges",
        compiler_params=room(8),
    )(*(far_off(x) for x in (coh, gx, gy, coh, gx, gy)))


def interior(coh, gx, gy):
    count, rows, cols = coh.shape
    tiles, blocks = (rows // 8, cols // 128)

    def body(c_hbm, x_hbm, y_hbm, r, v, u, wx, wy, extra, mom, cs, xs, ys, sems):
        half = rows // 2

        def copies(s):
            return [
                pltpu.make_async_copy(
                    src.at[:, pl.ds(s * half, half), pl.ds(128 * b, 128)],
                    dst.at[b, :, pl.ds(s * half, half), :],
                    sems.at[s, n, b],
                )
                for n, (src, dst) in enumerate(((c_hbm, cs), (x_hbm, xs), (y_hbm, ys)))
                for b in range(blocks)
            ]

        for s in range(2):
            for copy in copies(s):
                copy.start()

        def row_of(ref, i):
            return jnp.concatenate(
                [
                    ref.at[b].reshape(count * (rows + PAD), 128)[pl.ds(i, count, stride=rows + PAD), :]
                    for b in range(blocks)
                ],
                axis=1,
            )

        fy = jnp.zeros((count, cols), F32)
        for copy in copies(0):
            copy.wait()
        c = row_of(cs, 0)
        extra[0] = c
        for at in range(rows):
            if at == half - 1:
                for copy in copies(1):
                    copy.wait()
            w = col_weights(c)
            fx = w * row_of(xs, at)
            rhs = prev_col(fx) - fx + fy
            wx[at] = w
            if at < rows - 1:
                later = row_of(cs, at + 1)
                h = c * later
                wy[at] = h
                fy = h * row_of(ys, at)
                rhs = rhs - fy
                c = later
            else:
                wy[at] = jnp.zeros((count, cols), F32)
                extra[1] = c
                extra[2] = row_of(ys, at)
            r[at] = rhs

        def apply_to(src, dst, first, bound, near_bound):
            def tile(t, carry, low, high):
                fy, a, b = carry
                for i in range(8):
                    at = 8 * t + i
                    f = src[at]
                    after = src[jnp.minimum(at + 1, rows - 1)] if i == 7 else src[at + 1]
                    now = wy[at] * (f - after)
                    g = col_part(wx[at], f) + now - fy
                    fy = now
                    dst[at] = g
                    if low is None or low + i >= bound and high - i >= bound:
                        a = a + folded(f * f)
                    if low is None or low + i >= near_bound and high - i >= near_bound:
                        b = b + folded(f * g)
                return fy, a, b

            none = jnp.zeros((count, 128), F32)
            carry = (jnp.zeros((count, cols), F32), none, none)
            carry = tile(0, carry, 0, rows - 1)
            carry = lax.fori_loop(1, tiles - 1, lambda t, c: tile(t, c, None, None), carry)
            _, a, b = tile(tiles - 1, carry, rows - 8, 7)
            mom[first] = a
            mom[first + 1] = b

        apply_to(r, v, 0, 1, 2)
        apply_to(v, u, 2, 2, 3)

        def energy(t, carry, low, high):
            a, b = carry
            for i in range(8):
                if low is not None and (low + i < 3 or high - i < 3):
                    continue
                at = 8 * t + i
                f = u[at]
                d = f - next_col(f)
                e = wx[at] * d * d
                if low is None or high - i >= 4:
                    d = f - u[at + 1]
                    e = e + wy[at] * d * d
                a = a + folded(f * f)
                b = b + folded(e)
            return a, b

        none = jnp.zeros((count, 128), F32)
        carry = energy(0, (none, none), 0, rows - 1)
        carry = lax.fori_loop(1, tiles - 1, lambda t, c: energy(t, c, None, None), carry)
        mom[4], mom[5] = energy(tiles - 1, carry, rows - 8, 7)

    field = in_vmem(rows, count, cols)
    staged = pltpu.VMEM((blocks, count, rows + PAD, 128), F32)
    return pl.pallas_call(
        body,
        in_specs=[ANY] * 3,
        out_specs=[VMEM] * 7,
        out_shape=[field] * 5 + [in_vmem(3, count, cols), in_vmem(6, count, 128)],
        scratch_shapes=[staged] * 3 + [pltpu.SemaphoreType.DMA((2, 3, blocks))],
        name="interior",
        compiler_params=room(12),
    )(*(far_off(x) for x in (coh, gx, gy)))


def join(above, below, r, v, u, wx, wy, extra, mom):
    rows, count, cols = r.shape

    def body(ab, be, r_in, v_in, u_in, wx_ref, wy_ref, ex, m_in, r_out, v_out, u_out, out):
        end = rows - 1
        rr, vv, uu = ({}, {}, {})
        gx_w, gy_w = ({}, {})
        for i in (0, 1, 2, 3, end - 3, end - 2, end - 1, end):
            gx_w[i] = wx_ref[i]
            if i != end:
                gy_w[i] = wy_ref[i]
        gx_w[-1] = col_weights(ab[4])
        gy_w[-1] = ab[4] * ex[0]
        gy_w[-2] = ab[3] * ab[4]
        gy_w[end] = ex[1] * be[3]
        gy_w[end + 1] = be[3] * be[4]
        gy_w[end + 2] = be[4] * be[5]
        gx_w[end + 1] = col_weights(be[3])
        gx_w[end + 2] = col_weights(be[4])
        top = gy_w[-1] * ab[2]
        low = gy_w[end] * ex[2]
        rr[-2] = ab[0]
        rr[-1] = ab[1] - top
        rr[0] = r_in[0] + top
        rr[1], rr[2] = (r_in[1], r_in[2])
        rr[end - 2], rr[end - 1] = (r_in[end - 2], r_in[end - 1])
        rr[end] = r_in[end] - low
        rr[end + 1] = be[0] + low
        rr[end + 2] = be[1]
        rr[end + 3] = be[2]
        r_out[0] = rr[0]
        r_out[end] = rr[end]

        def applied(f, i):
            return (
                col_part(gx_w[i], f[i]) + gy_w[i] * (f[i] - f[i + 1]) - gy_w[i - 1] * (f[i - 1] - f[i])
            )

        sums = [m_in[j] for j in range(6)]

        def add(j, x):
            sums[j] = sums[j] + folded(x)

        for i in (-1, 0, 1, end - 1, end, end + 1, end + 2):
            vv[i] = applied(rr, i)
            if 0 <= i <= end:
                v_out[i] = vv[i]
        vv[2], vv[3] = (v_in[2], v_in[3])
        vv[end - 2], vv[end - 3] = (v_in[end - 2], v_in[end - 3])
        for i in (0, 1, 2, end - 2, end - 1, end, end + 1):
            uu[i] = applied(vv, i)
            if i <= end:
                u_out[i] = uu[i]
        uu[3], uu[end - 3] = (u_in[3], u_in[end - 3])
        for i in (0, end):
            add(0, rr[i] * rr[i])
        for i in (0, 1, end - 1, end):
            add(1, rr[i] * vv[i])
            add(2, vv[i] * vv[i])
        for i in (0, 1, 2, end - 2, end - 1, end):
            add(3, vv[i] * uu[i])
            add(4, uu[i] * uu[i])
            d = uu[i] - next_col(uu[i])
            h = uu[i] - uu[i + 1]
            add(5, gx_w[i] * d * d + gy_w[i] * h * h)
        h = uu[end - 3] - uu[end - 2]
        add(5, gy_w[end - 3] * h * h)
        lane = lax.broadcasted_iota(jnp.int32, (count, 128), 1)
        line = jnp.zeros((count, 128), F32)
        for j in range(6):
            line = jnp.where(lane == j, jnp.sum(sums[j], axis=1, keepdims=True), line)
        out[...] = line

    field = in_vmem(rows, count, cols)
    return pl.pallas_call(
        body,
        in_specs=[VMEM] * 9,
        out_specs=[VMEM] * 4,
        out_shape=[field] * 3 + [in_vmem(count, 128)],
        input_output_aliases={2: 0, 3: 1, 4: 2},
        name="join",
        compiler_params=room(4),
    )(near(above), near(below), r, v, u, wx, wy, extra, mom)


def iterate(r, v, u, shares, groups, widths):
    rows, count, cols = r.shape
    high = rows // groups
    number = len(shares)

    def body(*refs):
        r_ref, v_ref, u_ref = refs[:3]
        terms = [ref[...] for ref in refs[3 : 3 + number]]
        out, keep, beside, *far = refs[3 + number : -2]
        whole, sem = refs[-2:]
        while len(terms) > 1:
            terms = [sum(terms[i : i + 2][1:], terms[i]) for i in range(0, len(terms), 2)]
        m = terms[0]
        m0, m1, m2, m3, m4, m5 = (m[:, j : j + 1] for j in range(6))
        a00 = damping * m0 + m1
        a01 = damping * m1 + m2
        a02 = damping * m2 + m3
        a12 = damping * m3 + m4
        a22 = damping * m4 + m5

        def over(a, b, good):
            return jnp.where(good, a / jnp.where(good, b, 1.0), 0.0)

        ok0 = a00 > 0.0
        l10 = over(a01, a00, ok0)
        l20 = over(a02, a00, ok0)
        d1 = a02 - l10 * a01
        e12 = a12 - l10 * a02
        ok1 = d1 > TINY * a02
        l21 = over(e12, d1, ok1)
        d2 = a22 - l20 * a02 - l21 * e12
        ok2 = ok1 & (d2 > TINY * a22)
        y1 = m1 - l10 * m0
        y2 = m2 - l20 * m0 - l21 * y1
        c2 = over(y2, d2, ok2)
        c1 = over(y1, d1, ok1) - l21 * c2
        c0 = over(m0, a00, ok0) - l10 * c1 - l20 * c2
        c0, c1, c2 = (jnp.broadcast_to(c, (count, cols)) for c in (c0, c1, c2))
        _, me = half_and_member(groups)

        def put(ref, at, pitch, x):
            for b in range(ref.shape[0]):
                ref.at[b].reshape(count * pitch, 128)[pl.ds(at, count, stride=pitch), :] = x[
                    :, 128 * b : 128 * b + 128
                ]

        def rows_for(mask, pieces):
            first = jnp.bitwise_xor(me, mask) * high
            for a in range(high):
                at = first + a
                x = c0 * r_ref[at] + c1 * v_ref[at] + c2 * u_ref[at]
                put(whole, at, rows + PAD, x)
                left = 0
                for piece in pieces:
                    wide = 128 * piece.shape[0]
                    put(piece, a, high, x[:, left : left + wide])
                    left += wide

        rows_for(0, [keep])
        rows_for(1, [beside])
        for mask in range(2, groups):
            rows_for(mask, [far[(mask - 2) * len(widths) + i] for i in range(len(widths))])
        copies = [
            pltpu.make_async_copy(
                whole.at[b, :, pl.ds(0, rows), :], out.at[:, :, pl.ds(128 * b, 128)], sem.at[b]
            )
            for b in range(cols // 128)
        ]
        for copy in copies:
            copy.start()
        for copy in copies:
            copy.wait()

    return pl.pallas_call(
        body,
        in_specs=[VMEM] * (3 + number),
        out_specs=[ANY] + [VMEM] * (2 + (groups - 2) * len(widths)),
        out_shape=[jax.ShapeDtypeStruct((count, rows, cols), F32)]
        + [in_vmem(cols // 128, count, high, 128)] * 2
        + [in_vmem(wide // 128, count, high, 128) for _ in range(groups - 2) for wide in widths],
        scratch_shapes=[
            pltpu.VMEM((cols // 128, count, rows + PAD, 128), F32),
            pltpu.SemaphoreType.DMA((cols // 128,)),
        ],
        name="iterate",
        compiler_params=room(6),
    )(r, v, u, *(near(x) for x in shares))


def half_sums(mapping, left, fields, start=None):
    groups = len(fields)
    blocks, count, high, _ = fields[-1].shape
    dates = DATES // 2
    share = dates // groups
    spots = [(b, a) for b in range(blocks) for a in range(0, high, 8)]

    def body(map_ref, *refs):
        us = refs[:groups]

        def sums_of(ds, accs):
            for m in range(groups):
                base = 0 if us[m].shape[0] == blocks else left // 128
                for k in range(count):
                    column = m * count + k
                    ws = [map_ref[d, column] for d in ds]
                    for i, (b, a) in enumerate(spots):
                        u = us[m][base + b, k, a : a + 8, :]
                        for acc, w in zip(accs, ws):
                            acc[i] = acc[i] + w * u
            return accs

        def store(out, d, acc):
            for (b, a), x in zip(spots, acc):
                out[b, d, a : a + 8, :] = x

        def pair_of(first, out, begin):
            def step(i, _):
                at = [2 * i, 2 * i + 1]
                for d, acc in zip(at, sums_of([first + d for d in at], [begin(d) for d in at])):
                    store(out, d, acc)
                return 0

            return step

        if start is None:
            none = lambda d: [jnp.zeros((8, 128), F32) for _ in spots]
            lax.fori_loop(0, dates // 2, pair_of(0, refs[groups], none), 0)
        else:
            me = half_and_member(groups)[1]
            begun = refs[groups]
            for m, out in enumerate(refs[groups + 1 :]):
                first = jnp.bitwise_xor(me, m) * share
                begin = lambda d, first=first: [begun[b, first + d, a : a + 8, :] for b, a in spots]
                lax.fori_loop(0, share // 2, pair_of(dates + m * share, out, begin), 0)

    args = list(fields) + ([] if start is None else [start])
    out_shape = (
        [in_vmem(blocks, dates, high, 128)]
        if start is None
        else [in_vmem(blocks, share, high, 128)] * groups
    )
    return pl.pallas_call(
        body,
        in_specs=[SMEM] + [VMEM] * len(args),
        out_specs=[VMEM] * len(out_shape),
        out_shape=out_shape,
        name="cross_sums" if start is None else "own_sums",
        compiler_params=room(4),
    )(mapping, *(near(x) for x in args))


def assemble(parts, rows, cols):
    groups = len(parts[0])
    _, dates, high, _ = parts[0][0].shape
    flat = [x for chunk in parts for x in chunk]

    def body(*refs):
        _, me = half_and_member(groups)
        out = refs[-1]
        left = 0
        for i in range(len(parts)):
            blocks = parts[i][0].shape[0]
            for m in range(groups):
                first = pl.multiple_of(jnp.bitwise_xor(me, m) * high, 8)
                for b in range(blocks):
                    at = left + 128 * b
                    out[:, pl.ds(first, high), at : at + 128] = refs[i * groups + m][b]
            left += 128 * blocks

    return pl.pallas_call(
        body,
        in_specs=[VMEM] * len(flat),
        out_specs=VMEM,
        out_shape=jax.ShapeDtypeStruct((dates, rows, cols), F32),
        name="assemble",
        compiler_params=room(4),
    )(*(near(x) for x in flat))


def exchange(x, axis, mask):
    size = lax.axis_size(axis)
    return lax.ppermute(x, axis, [(i, i ^ mask) for i in range(size)])


def summands(x, axis):
    size, bit, terms = (lax.axis_size(axis), 1, [x])
    while bit < size:
        if len(terms) > 1:
            terms = [(terms[0] + terms[1]) + (terms[2] + terms[3])]
        masks = [bit, 2 * bit, 3 * bit] if 4 * bit <= size else [bit]
        terms = terms + [exchange(terms[0], axis, m) for m in masks]
        bit *= len(masks) + 1
    return terms


def on_device(grad_x, grad_y, coherence, pairs):
    strips, size = (lax.axis_size("strip"), lax.axis_size("ifg"))
    _, rows, cols = coherence.shape
    groups = size // 2
    widths = [cols * part // sum(SLICES) for part in SLICES]
    down, up = edges(coherence, grad_x, grad_y)
    forward = [(i, i + 1) for i in range(strips - 1)]
    above = lax.ppermute(down, "strip", forward)
    below = lax.ppermute(up, "strip", [(j, i) for i, j in forward])
    fields = interior(coherence, grad_x, grad_y)
    r, v, u, moments = join(above, below, *fields)
    shares = summands(moments, "strip")
    mapping = inverse_map(pairs, groups)
    phase, keep, beside, *far = iterate(r, v, u, shares, groups, widths)
    beside = exchange(beside, "ifg", 1)
    parts, left = ([], 0)
    for i, wide in enumerate(widths):
        mine = [keep, beside]
        for m in range(2, groups):
            mine.append(exchange(far[(m - 2) * CHUNKS + i], "ifg", m))
        (other,) = half_sums(mapping, left, mine)
        other = exchange(other, "ifg", groups)
        full = half_sums(mapping, left, mine, other)
        part = [full[0]]
        for m in range(1, groups):
            part.append(exchange(full[m], "ifg", m))
        parts.append(part)
        left += wide
    return (phase, assemble(parts, rows, cols))


def solution(mesh):
    in_specs = (P("ifg", "strip", None), P("ifg", "strip", None), P("ifg", "strip", None), P())
    out_specs = (P("ifg", "strip", None), P("ifg", "strip", None))

    return jax.shard_map(on_device, mesh=mesh, in_specs=in_specs, out_specs=out_specs, check_vma=False)
```

```python
import jax
import jax.numpy as jnp
from jax import lax
from jax.experimental import pallas as pl
from jax.experimental.pallas import tpu as pltpu
from jax.sharding import PartitionSpec as P

DATES = 32
SLICES = (1, 2, 2, 2, 1)
CHUNKS = len(SLICES)
PAD = 8
damping = 0.1
TINY = 1e-6
F32 = jnp.float32
ANY = pl.BlockSpec(memory_space=pl.ANY)
SMEM = pl.BlockSpec(memory_space=pltpu.SMEM)
VMEM = pl.BlockSpec(memory_space=pltpu.VMEM)


def room(mib):
    return pltpu.CompilerParams(vmem_limit_bytes=mib * 2**20)


def near(x):
    return pltpu.with_memory_space_constraint(x, pltpu.VMEM)


def far_off(x):
    return pltpu.with_memory_space_constraint(x, pltpu.HBM)


def half_and_member(groups):
    index = lax.axis_index("ifg").astype(jnp.int32)
    return (index // groups, index % groups)


def in_vmem(*shape):
    return pltpu.VMEM(shape, F32)


def turned_cols(x, by, at):
    lane = lax.broadcasted_iota(jnp.int32, (x.shape[0], 128), 1)
    turned = [pltpu.roll(x[:, i : i + 128], by % 128, axis=1) for i in range(0, x.shape[1], 128)]
    moved = turned[-by:] + turned[:-by]
    return jnp.concatenate([jnp.where(lane == at, m, t) for m, t in zip(moved, turned)], axis=1)


def next_col(x):
    return turned_cols(x, -1, 127)


def prev_col(x):
    return turned_cols(x, 1, 0)


def col_weights(c):
    lane = lax.broadcasted_iota(jnp.int32, c.shape, 1)
    return jnp.where(lane < c.shape[1] - 1, c * next_col(c), 0.0)


def col_part(w, f):
    fx = w * (f - next_col(f))
    return fx - prev_col(fx)


def folded(x):
    parts = [x[:, i : i + 128] for i in range(0, x.shape[1], 128)]
    while len(parts) > 1:
        parts = [sum(parts[i : i + 2][1:], parts[i]) for i in range(0, len(parts), 2)]
    return parts[0]


def inverse_map(pairs, groups):
    number = pairs.shape[0]
    inner = number // 2
    wide = -(-(DATES + number) // 128) * 128
    share = DATES // (2 * groups)
    count = number // (2 * groups)

    def body(pair, out, work):
        h, me = half_and_member(groups)

        def twin(i, each):
            return jnp.bitwise_xor(i // each, me) * each + i % each

        d = lax.broadcasted_iota(jnp.int32, (DATES, number), 0)
        half = DATES // 2
        slots = jnp.where(d < half, (1 - h) * half + d, h * half + twin(d % half, share))
        k = lax.broadcasted_iota(jnp.int32, (number, number), 1)
        source = jnp.where(k < inner, h * inner + twin(k % inner, count), (1 - h) * inner + k % inner)
        turn = (source == lax.broadcasted_iota(jnp.int32, (number, number), 0)).astype(F32)
        p = jnp.dot(
            pair[...].astype(F32), turn, precision=lax.Precision.HIGHEST, preferred_element_type=F32
        )
        slots = slots.astype(F32)
        back = (p[1:2] == slots).astype(F32) - (p[0:1] == slots).astype(F32)
        normal = 1.0 + lax.dot_general(
            back, back, (((1,), (1,)), ((), ())), precision=lax.Precision.HIGHEST, preferred_element_type=F32
        )
        work[...] = jnp.zeros_like(work)
        work[:, :DATES] = normal
        work[:, DATES : DATES + number] = back
        w = work[...]
        row = lax.broadcasted_iota(jnp.int32, (DATES, wide), 0)
        for j in range(DATES):
            pivot = w[j : j + 1] / w[j : j + 1, j : j + 1]
            w = jnp.where(row == j, pivot, w - w[:, j : j + 1] * pivot)
        work[...] = w
        out[...] = work[:, DATES : DATES + inner]

    return pl.pallas_call(
        body,
        in_specs=[VMEM],
        out_specs=VMEM,
        out_shape=jax.ShapeDtypeStruct((DATES, inner), F32),
        scratch_shapes=[pltpu.VMEM((DATES, wide), F32)],
        name="inverse_map",
        compiler_params=room(2),
    )(pairs.T)


def edges(coh, gx, gy):
    count, rows, cols = coh.shape
    last_tile = rows // 8 - 1

    def body(ct, xt, yt, cb, xb, yb, first, second):
        row = lax.broadcasted_iota(jnp.int32, (8, cols), 0)

        def partial_rhs(c, x, y):
            fx = col_weights(c) * x
            fy = jnp.where(row < 7, c * pltpu.roll(c, 7, axis=0) * y, 0.0)
            return -(fx - prev_col(fx) + fy - pltpu.roll(fy, 1, axis=0))

        def send(down, up):
            for k in range(count):
                c, y = (cb[k], yb[k])
                r = partial_rhs(c, xb[k], y)
                for i, x in enumerate((r[6:7], r[7:8], y[7:8], c[6:7], c[7:8])):
                    down[i, k : k + 1, :] = x
                c = ct[k]
                r = partial_rhs(c, xt[k], yt[k])
                for i in range(3):
                    up[i, k : k + 1, :] = r[i : i + 1]
                    up[3 + i, k : k + 1, :] = c[i : i + 1]
            down[5] = jnp.zeros((count, cols), F32)

        even = lax.axis_index("strip") % 2 == 0

        @pl.when(even)
        def _():
            send(first, second)

        @pl.when(jnp.logical_not(even))
        def _():
            send(second, first)

    top = pl.BlockSpec((count, 8, cols), lambda i: (0, 0, 0))
    bottom = pl.BlockSpec((count, 8, cols), lambda i: (0, last_tile, 0))
    return pl.pallas_call(
        body,
        grid=(1,),
        in_specs=[top, top, top, bottom, bottom, bottom],
        out_specs=[
            pl.BlockSpec((6, count, cols), lambda i: (0, 0, 0)),
            pl.BlockSpec((6, count, cols), lambda i: (0, 0, 0)),
        ],
        out_shape=[
            jax.ShapeDtypeStruct((6, count, cols), F32),
            jax.ShapeDtypeStruct((6, count, cols), F32),
        ],
        name="edges",
        compiler_params=room(8),
    )(*(far_off(x) for x in (coh, gx, gy, coh, gx, gy)))


def interior(coh, gx, gy):
    count, rows, cols = coh.shape
    tiles, blocks = (rows // 8, cols // 128)

    def body(c_hbm, x_hbm, y_hbm, r, v, u, wx, wy, extra, mom, cs, xs, ys, sems):
        half = rows // 2

        def copies(s):
            return [
                pltpu.make_async_copy(
                    src.at[:, pl.ds(s * half, half), pl.ds(128 * b, 128)],
                    dst.at[b, :, pl.ds(s * half, half), :],
                    sems.at[s, n, b],
                )
                for n, (src, dst) in enumerate(((c_hbm, cs), (x_hbm, xs), (y_hbm, ys)))
                for b in range(blocks)
            ]

        for s in range(2):
            for copy in copies(s):
                copy.start()

        def row_of(ref, i):
            return jnp.concatenate(
                [
                    ref.at[b].reshape(count * (rows + PAD), 128)[pl.ds(i, count, stride=rows + PAD), :]
                    for b in range(blocks)
                ],
                axis=1,
            )

        fy = jnp.zeros((count, cols), F32)
        for copy in copies(0):
            copy.wait()
        c = row_of(cs, 0)
        extra[0] = c
        for at in range(rows):
            if at == half - 1:
                for copy in copies(1):
                    copy.wait()
            w = col_weights(c)
            fx = w * row_of(xs, at)
            rhs = prev_col(fx) - fx + fy
            wx[at] = w
            if at < rows - 1:
                later = row_of(cs, at + 1)
                h = c * later
                wy[at] = h
                fy = h * row_of(ys, at)
                rhs = rhs - fy
                c = later
            else:
                wy[at] = jnp.zeros((count, cols), F32)
                extra[1] = c
                extra[2] = row_of(ys, at)
            r[at] = rhs

        def apply_to(src, dst, first, bound, near_bound):
            def tile(t, carry, low, high):
                fy, a, b = carry
                for i in range(8):
                    at = 8 * t + i
                    f = src[at]
                    after = src[jnp.minimum(at + 1, rows - 1)] if i == 7 else src[at + 1]
                    now = wy[at] * (f - after)
                    g = col_part(wx[at], f) + now - fy
                    fy = now
                    dst[at] = g
                    if low is None or low + i >= bound and high - i >= bound:
                        a = a + folded(f * f)
                    if low is None or low + i >= near_bound and high - i >= near_bound:
                        b = b + folded(f * g)
                return fy, a, b

            none = jnp.zeros((count, 128), F32)
            carry = (jnp.zeros((count, cols), F32), none, none)
            carry = tile(0, carry, 0, rows - 1)
            carry = lax.fori_loop(1, tiles - 1, lambda t, c: tile(t, c, None, None), carry)
            _, a, b = tile(tiles - 1, carry, rows - 8, 7)
            mom[first] = a
            mom[first + 1] = b

        apply_to(r, v, 0, 1, 2)
        apply_to(v, u, 2, 2, 3)

        def energy(t, carry, low, high):
            a, b = carry
            for i in range(8):
                if low is not None and (low + i < 3 or high - i < 3):
                    continue
                at = 8 * t + i
                f = u[at]
                d = f - next_col(f)
                e = wx[at] * d * d
                if low is None or high - i >= 4:
                    d = f - u[at + 1]
                    e = e + wy[at] * d * d
                a = a + folded(f * f)
                b = b + folded(e)
            return a, b

        none = jnp.zeros((count, 128), F32)
        carry = energy(0, (none, none), 0, rows - 1)
        carry = lax.fori_loop(1, tiles - 1, lambda t, c: energy(t, c, None, None), carry)
        mom[4], mom[5] = energy(tiles - 1, carry, rows - 8, 7)

    field = in_vmem(rows, count, cols)
    staged = pltpu.VMEM((blocks, count, rows + PAD, 128), F32)
    return pl.pallas_call(
        body,
        in_specs=[ANY] * 3,
        out_specs=[VMEM] * 7,
        out_shape=[field] * 5 + [in_vmem(3, count, cols), in_vmem(6, count, 128)],
        scratch_shapes=[staged] * 3 + [pltpu.SemaphoreType.DMA((2, 3, blocks))],
        name="interior",
        compiler_params=room(12),
    )(*(far_off(x) for x in (coh, gx, gy)))


def join(first, second, r, v, u, wx, wy, extra, mom):
    rows, count, cols = r.shape

    def body(got_first, got_second, r_in, v_in, u_in, wx_ref, wy_ref, ex, m_in, r_out, v_out, u_out, out):
        end = rows - 1
        even = lax.axis_index("strip") % 2 == 0
        ab = [jnp.where(even, got_second[i], got_first[i]) for i in range(5)]
        be = [jnp.where(even, got_first[i], got_second[i]) for i in range(6)]
        rr, vv, uu = ({}, {}, {})
        gx_w, gy_w = ({}, {})
        for i in (0, 1, 2, 3, end - 3, end - 2, end - 1, end):
            gx_w[i] = wx_ref[i]
            if i != end:
                gy_w[i] = wy_ref[i]
        gx_w[-1] = col_weights(ab[4])
        gy_w[-1] = ab[4] * ex[0]
        gy_w[-2] = ab[3] * ab[4]
        gy_w[end] = ex[1] * be[3]
        gy_w[end + 1] = be[3] * be[4]
        gy_w[end + 2] = be[4] * be[5]
        gx_w[end + 1] = col_weights(be[3])
        gx_w[end + 2] = col_weights(be[4])
        top = gy_w[-1] * ab[2]
        low = gy_w[end] * ex[2]
        rr[-2] = ab[0]
        rr[-1] = ab[1] - top
        rr[0] = r_in[0] + top
        rr[1], rr[2] = (r_in[1], r_in[2])
        rr[end - 2], rr[end - 1] = (r_in[end - 2], r_in[end - 1])
        rr[end] = r_in[end] - low
        rr[end + 1] = be[0] + low
        rr[end + 2] = be[1]
        rr[end + 3] = be[2]
        r_out[0] = rr[0]
        r_out[end] = rr[end]

        def applied(f, i):
            return (
                col_part(gx_w[i], f[i]) + gy_w[i] * (f[i] - f[i + 1]) - gy_w[i - 1] * (f[i - 1] - f[i])
            )

        sums = [m_in[j] for j in range(6)]

        def add(j, x):
            sums[j] = sums[j] + folded(x)

        for i in (-1, 0, 1, end - 1, end, end + 1, end + 2):
            vv[i] = applied(rr, i)
            if 0 <= i <= end:
                v_out[i] = vv[i]
        vv[2], vv[3] = (v_in[2], v_in[3])
        vv[end - 2], vv[end - 3] = (v_in[end - 2], v_in[end - 3])
        for i in (0, 1, 2, end - 2, end - 1, end, end + 1):
            uu[i] = applied(vv, i)
            if i <= end:
                u_out[i] = uu[i]
        uu[3], uu[end - 3] = (u_in[3], u_in[end - 3])
        for i in (0, end):
            add(0, rr[i] * rr[i])
        for i in (0, 1, end - 1, end):
            add(1, rr[i] * vv[i])
            add(2, vv[i] * vv[i])
        for i in (0, 1, 2, end - 2, end - 1, end):
            add(3, vv[i] * uu[i])
            add(4, uu[i] * uu[i])
            d = uu[i] - next_col(uu[i])
            h = uu[i] - uu[i + 1]
            add(5, gx_w[i] * d * d + gy_w[i] * h * h)
        h = uu[end - 3] - uu[end - 2]
        add(5, gy_w[end - 3] * h * h)
        lane = lax.broadcasted_iota(jnp.int32, (count, 128), 1)
        line = jnp.zeros((count, 128), F32)
        for j in range(6):
            line = jnp.where(lane == j, jnp.sum(sums[j], axis=1, keepdims=True), line)
        out[...] = line

    field = in_vmem(rows, count, cols)
    return pl.pallas_call(
        body,
        in_specs=[VMEM] * 9,
        out_specs=[VMEM] * 4,
        out_shape=[field] * 3 + [in_vmem(count, 128)],
        input_output_aliases={2: 0, 3: 1, 4: 2},
        name="join",
        compiler_params=room(4),
    )(near(first), near(second), r, v, u, wx, wy, extra, mom)


def iterate(r, v, u, shares, groups, widths):
    rows, count, cols = r.shape
    high = rows // groups
    number = len(shares)

    def body(*refs):
        r_ref, v_ref, u_ref = refs[:3]
        terms = [ref[...] for ref in refs[3 : 3 + number]]
        out, keep, beside, *far = refs[3 + number : -2]
        whole, sem = refs[-2:]
        while len(terms) > 1:
            terms = [sum(terms[i : i + 2][1:], terms[i]) for i in range(0, len(terms), 2)]
        m = terms[0]
        m0, m1, m2, m3, m4, m5 = (m[:, j : j + 1] for j in range(6))
        a00 = damping * m0 + m1
        a01 = damping * m1 + m2
        a02 = damping * m2 + m3
        a12 = damping * m3 + m4
        a22 = damping * m4 + m5

        def over(a, b, good):
            return jnp.where(good, a / jnp.where(good, b, 1.0), 0.0)

        ok0 = a00 > 0.0
        l10 = over(a01, a00, ok0)
        l20 = over(a02, a00, ok0)
        d1 = a02 - l10 * a01
        e12 = a12 - l10 * a02
        ok1 = d1 > TINY * a02
        l21 = over(e12, d1, ok1)
        d2 = a22 - l20 * a02 - l21 * e12
        ok2 = ok1 & (d2 > TINY * a22)
        y1 = m1 - l10 * m0
        y2 = m2 - l20 * m0 - l21 * y1
        c2 = over(y2, d2, ok2)
        c1 = over(y1, d1, ok1) - l21 * c2
        c0 = over(m0, a00, ok0) - l10 * c1 - l20 * c2
        c0, c1, c2 = (jnp.broadcast_to(c, (count, cols)) for c in (c0, c1, c2))
        _, me = half_and_member(groups)

        def put(ref, at, pitch, x):
            for b in range(ref.shape[0]):
                ref.at[b].reshape(count * pitch, 128)[pl.ds(at, count, stride=pitch), :] = x[
                    :, 128 * b : 128 * b + 128
                ]

        def rows_for(mask, pieces):
            first = jnp.bitwise_xor(me, mask) * high
            for a in range(high):
                at = first + a
                x = c0 * r_ref[at] + c1 * v_ref[at] + c2 * u_ref[at]
                put(whole, at, rows + PAD, x)
                left = 0
                for piece in pieces:
                    wide = 128 * piece.shape[0]
                    put(piece, a, high, x[:, left : left + wide])
                    left += wide

        rows_for(0, [keep])
        rows_for(1, [beside])
        for mask in range(2, groups):
            rows_for(mask, [far[(mask - 2) * len(widths) + i] for i in range(len(widths))])
        copies = [
            pltpu.make_async_copy(
                whole.at[b, :, pl.ds(0, rows), :], out.at[:, :, pl.ds(128 * b, 128)], sem.at[b]
            )
            for b in range(cols // 128)
        ]
        for copy in copies:
            copy.start()
        for copy in copies:
            copy.wait()

    return pl.pallas_call(
        body,
        in_specs=[VMEM] * (3 + number),
        out_specs=[ANY] + [VMEM] * (2 + (groups - 2) * len(widths)),
        out_shape=[jax.ShapeDtypeStruct((count, rows, cols), F32)]
        + [in_vmem(cols // 128, count, high, 128)] * 2
        + [in_vmem(wide // 128, count, high, 128) for _ in range(groups - 2) for wide in widths],
        scratch_shapes=[
            pltpu.VMEM((cols // 128, count, rows + PAD, 128), F32),
            pltpu.SemaphoreType.DMA((cols // 128,)),
        ],
        name="iterate",
        compiler_params=room(6),
    )(r, v, u, *(near(x) for x in shares))


def half_sums(mapping, left, fields, start=None):
    groups = len(fields)
    blocks, count, high, _ = fields[-1].shape
    dates = DATES // 2
    share = dates // groups
    spots = [(b, a) for b in range(blocks) for a in range(0, high, 8)]

    def body(map_ref, *refs):
        us = refs[:groups]

        def sums_of(ds, accs):
            for m in range(groups):
                base = 0 if us[m].shape[0] == blocks else left // 128
                for k in range(count):
                    column = m * count + k
                    ws = [map_ref[d, column] for d in ds]
                    for i, (b, a) in enumerate(spots):
                        u = us[m][base + b, k, a : a + 8, :]
                        for acc, w in zip(accs, ws):
                            acc[i] = acc[i] + w * u
            return accs

        def store(out, d, acc):
            for (b, a), x in zip(spots, acc):
                out[b, d, a : a + 8, :] = x

        def pair_of(first, out, begin):
            def step(i, _):
                at = [2 * i, 2 * i + 1]
                for d, acc in zip(at, sums_of([first + d for d in at], [begin(d) for d in at])):
                    store(out, d, acc)
                return 0

            return step

        if start is None:
            none = lambda d: [jnp.zeros((8, 128), F32) for _ in spots]
            lax.fori_loop(0, dates // 2, pair_of(0, refs[groups], none), 0)
        else:
            me = half_and_member(groups)[1]
            begun = refs[groups]
            for m, out in enumerate(refs[groups + 1 :]):
                first = jnp.bitwise_xor(me, m) * share
                begin = lambda d, first=first: [begun[b, first + d, a : a + 8, :] for b, a in spots]
                lax.fori_loop(0, share // 2, pair_of(dates + m * share, out, begin), 0)

    args = list(fields) + ([] if start is None else [start])
    out_shape = (
        [in_vmem(blocks, dates, high, 128)]
        if start is None
        else [in_vmem(blocks, share, high, 128)] * groups
    )
    return pl.pallas_call(
        body,
        in_specs=[SMEM] + [VMEM] * len(args),
        out_specs=[VMEM] * len(out_shape),
        out_shape=out_shape,
        name="cross_sums" if start is None else "own_sums",
        compiler_params=room(4),
    )(mapping, *(near(x) for x in args))


def assemble(parts, rows, cols):
    groups = len(parts[0])
    _, dates, high, _ = parts[0][0].shape
    flat = [x for chunk in parts for x in chunk]

    def body(*refs):
        _, me = half_and_member(groups)
        out = refs[-1]
        left = 0
        for i in range(len(parts)):
            blocks = parts[i][0].shape[0]
            for m in range(groups):
                first = pl.multiple_of(jnp.bitwise_xor(me, m) * high, 8)
                for b in range(blocks):
                    at = left + 128 * b
                    out[:, pl.ds(first, high), at : at + 128] = refs[i * groups + m][b]
            left += 128 * blocks

    return pl.pallas_call(
        body,
        in_specs=[VMEM] * len(flat),
        out_specs=VMEM,
        out_shape=jax.ShapeDtypeStruct((dates, rows, cols), F32),
        name="assemble",
        compiler_params=room(4),
    )(*(near(x) for x in flat))


def exchange(x, axis, mask):
    size = lax.axis_size(axis)
    return lax.ppermute(x, axis, [(i, i ^ mask) for i in range(size)])


def summands(x, axis):
    size, bit, terms = (lax.axis_size(axis), 1, [x])
    while bit < size:
        if len(terms) > 1:
            terms = [(terms[0] + terms[1]) + (terms[2] + terms[3])]
        masks = [bit, 2 * bit, 3 * bit] if 4 * bit <= size else [bit]
        terms = terms + [exchange(terms[0], axis, m) for m in masks]
        bit *= len(masks) + 1
    return terms


def on_device(grad_x, grad_y, coherence, pairs):
    strips, size = (lax.axis_size("strip"), lax.axis_size("ifg"))
    _, rows, cols = coherence.shape
    groups = size // 2
    widths = [cols * part // sum(SLICES) for part in SLICES]
    first, second = edges(coherence, grad_x, grad_y)
    first, second = (
        lax.ppermute(x, "strip", [p for i in range(at, strips - 1, 2) for p in ((i, i + 1), (i + 1, i))])
        for at, x in enumerate((first, second))
    )
    fields = interior(coherence, grad_x, grad_y)
    r, v, u, moments = join(first, second, *fields)
    shares = summands(moments, "strip")
    mapping = inverse_map(pairs, groups)
    phase, keep, beside, *far = iterate(r, v, u, shares, groups, widths)
    beside = exchange(beside, "ifg", 1)
    parts, left = ([], 0)
    for i, wide in enumerate(widths):
        mine = [keep, beside]
        for m in range(2, groups):
            mine.append(exchange(far[(m - 2) * CHUNKS + i], "ifg", m))
        (other,) = half_sums(mapping, left, mine)
        other = exchange(other, "ifg", groups)
        full = half_sums(mapping, left, mine, other)
        part = [full[0]]
        for m in range(1, groups):
            part.append(exchange(full[m], "ifg", m))
        parts.append(part)
        left += wide
    return (phase, assemble(parts, rows, cols))


def solution(mesh):
    in_specs = (P("ifg", "strip", None), P("ifg", "strip", None), P("ifg", "strip", None), P())
    out_specs = (P("ifg", "strip", None), P("ifg", "strip", None))

    return jax.shard_map(on_device, mesh=mesh, in_specs=in_specs, out_specs=out_specs, check_vma=False)
```

```python
import jax
import jax.numpy as jnp
from jax import lax
from jax.experimental import pallas as pl
from jax.experimental.pallas import tpu as pltpu
from jax.sharding import PartitionSpec as P

DATES = 32
SLICES = (1, 2, 2, 2, 1)
CHUNKS = len(SLICES)
PAD = 8
damping = 0.1
TINY = 1e-6
F32 = jnp.float32
ANY = pl.BlockSpec(memory_space=pl.ANY)
SMEM = pl.BlockSpec(memory_space=pltpu.SMEM)
VMEM = pl.BlockSpec(memory_space=pltpu.VMEM)


def room(mib):
    return pltpu.CompilerParams(vmem_limit_bytes=mib * 2**20)


def near(x):
    return pltpu.with_memory_space_constraint(x, pltpu.VMEM)


def far_off(x):
    return pltpu.with_memory_space_constraint(x, pltpu.HBM)


def half_and_member(groups):
    index = lax.axis_index("ifg").astype(jnp.int32)
    return (index // groups, index % groups)


def in_vmem(*shape):
    return pltpu.VMEM(shape, F32)


def turned_cols(x, by, at):
    lane = lax.broadcasted_iota(jnp.int32, (x.shape[0], 128), 1)
    turned = [pltpu.roll(x[:, i : i + 128], by % 128, axis=1) for i in range(0, x.shape[1], 128)]
    moved = turned[-by:] + turned[:-by]
    return jnp.concatenate([jnp.where(lane == at, m, t) for m, t in zip(moved, turned)], axis=1)


def next_col(x):
    return turned_cols(x, -1, 127)


def prev_col(x):
    return turned_cols(x, 1, 0)


def col_weights(c):
    lane = lax.broadcasted_iota(jnp.int32, c.shape, 1)
    return jnp.where(lane < c.shape[1] - 1, c * next_col(c), 0.0)


def col_part(w, f):
    fx = w * (f - next_col(f))
    return fx - prev_col(fx)


def folded(x):
    parts = [x[:, i : i + 128] for i in range(0, x.shape[1], 128)]
    while len(parts) > 1:
        parts = [sum(parts[i : i + 2][1:], parts[i]) for i in range(0, len(parts), 2)]
    return parts[0]


def inverse_map(pairs, groups):
    number = pairs.shape[0]
    inner = number // 2
    wide = -(-(DATES + number) // 128) * 128
    share = DATES // (2 * groups)
    count = number // (2 * groups)

    def body(pair, out, work):
        h, me = half_and_member(groups)

        def twin(i, each):
            return jnp.bitwise_xor(i // each, me) * each + i % each

        d = lax.broadcasted_iota(jnp.int32, (DATES, number), 0)
        half = DATES // 2
        slots = jnp.where(d < half, (1 - h) * half + d, h * half + twin(d % half, share))
        k = lax.broadcasted_iota(jnp.int32, (number, number), 1)
        source = jnp.where(k < inner, h * inner + twin(k % inner, count), (1 - h) * inner + k % inner)
        turn = (source == lax.broadcasted_iota(jnp.int32, (number, number), 0)).astype(F32)
        p = jnp.dot(
            pair[...].astype(F32), turn, precision=lax.Precision.HIGHEST, preferred_element_type=F32
        )
        slots = slots.astype(F32)
        back = (p[1:2] == slots).astype(F32) - (p[0:1] == slots).astype(F32)
        normal = 1.0 + lax.dot_general(
            back, back, (((1,), (1,)), ((), ())), precision=lax.Precision.HIGHEST, preferred_element_type=F32
        )
        work[...] = jnp.zeros_like(work)
        work[:, :DATES] = normal
        work[:, DATES : DATES + number] = back
        w = work[...]
        row = lax.broadcasted_iota(jnp.int32, (DATES, wide), 0)
        for j in range(DATES):
            pivot = w[j : j + 1] / w[j : j + 1, j : j + 1]
            w = jnp.where(row == j, pivot, w - w[:, j : j + 1] * pivot)
        work[...] = w
        out[...] = work[:, DATES : DATES + inner]

    return pl.pallas_call(
        body,
        in_specs=[VMEM],
        out_specs=VMEM,
        out_shape=jax.ShapeDtypeStruct((DATES, inner), F32),
        scratch_shapes=[pltpu.VMEM((DATES, wide), F32)],
        name="inverse_map",
        compiler_params=room(2),
    )(pairs.T)


def edges(coh, gx, gy):
    count, rows, cols = coh.shape
    last_tile = rows // 8 - 1

    def body(ct, xt, yt, cb, xb, yb, first, second):
        row = lax.broadcasted_iota(jnp.int32, (8, cols), 0)

        def partial_rhs(c, x, y):
            fx = col_weights(c) * x
            fy = jnp.where(row < 7, c * pltpu.roll(c, 7, axis=0) * y, 0.0)
            return -(fx - prev_col(fx) + fy - pltpu.roll(fy, 1, axis=0))

        def send(down, up):
            for k in range(count):
                c, y = (cb[k], yb[k])
                r = partial_rhs(c, xb[k], y)
                for i, x in enumerate((r[6:7], r[7:8], y[7:8], c[6:7], c[7:8])):
                    down[i, k : k + 1, :] = x
                c = ct[k]
                r = partial_rhs(c, xt[k], yt[k])
                for i in range(3):
                    up[i, k : k + 1, :] = r[i : i + 1]
                    up[3 + i, k : k + 1, :] = c[i : i + 1]
            down[5] = jnp.zeros((count, cols), F32)

        even = lax.axis_index("strip") % 2 == 0

        @pl.when(even)
        def _():
            send(first, second)

        @pl.when(jnp.logical_not(even))
        def _():
            send(second, first)

    top = pl.BlockSpec((count, 8, cols), lambda i: (0, 0, 0))
    bottom = pl.BlockSpec((count, 8, cols), lambda i: (0, last_tile, 0))
    return pl.pallas_call(
        body,
        grid=(1,),
        in_specs=[top, top, top, bottom, bottom, bottom],
        out_specs=[
            pl.BlockSpec((6, count, cols), lambda i: (0, 0, 0)),
            pl.BlockSpec((6, count, cols), lambda i: (0, 0, 0)),
        ],
        out_shape=[
            jax.ShapeDtypeStruct((6, count, cols), F32),
            jax.ShapeDtypeStruct((6, count, cols), F32),
        ],
        name="edges",
        compiler_params=room(8),
    )(*(far_off(x) for x in (coh, gx, gy, coh, gx, gy)))


def interior(coh, gx, gy):
    count, rows, cols = coh.shape
    tiles, blocks = (rows // 8, cols // 128)

    def body(c_hbm, x_hbm, y_hbm, r, v, u, wx, wy, extra, mom, cs, xs, ys, sems):
        half = rows // 2

        def copies(s):
            return [
                pltpu.make_async_copy(
                    src.at[:, pl.ds(s * half, half), pl.ds(128 * b, 128)],
                    dst.at[b, :, pl.ds(s * half, half), :],
                    sems.at[s, n, b],
                )
                for n, (src, dst) in enumerate(((c_hbm, cs), (x_hbm, xs), (y_hbm, ys)))
                for b in range(blocks)
            ]

        for s in range(2):
            for copy in copies(s):
                copy.start()

        def row_of(ref, i):
            return jnp.concatenate(
                [
                    ref.at[b].reshape(count * (rows + PAD), 128)[pl.ds(i, count, stride=rows + PAD), :]
                    for b in range(blocks)
                ],
                axis=1,
            )

        fy = jnp.zeros((count, cols), F32)
        for copy in copies(0):
            copy.wait()
        c = row_of(cs, 0)
        extra[0] = c
        for at in range(rows):
            if at == half - 1:
                for copy in copies(1):
                    copy.wait()
            w = col_weights(c)
            fx = w * row_of(xs, at)
            rhs = prev_col(fx) - fx + fy
            wx[at] = w
            if at < rows - 1:
                later = row_of(cs, at + 1)
                h = c * later
                wy[at] = h
                fy = h * row_of(ys, at)
                rhs = rhs - fy
                c = later
            else:
                wy[at] = jnp.zeros((count, cols), F32)
                extra[1] = c
                extra[2] = row_of(ys, at)
            r[at] = rhs

        def apply_to(src, dst, first, bound, near_bound):
            def tile(t, carry, low, high):
                fy, a, b = carry
                for i in range(8):
                    at = 8 * t + i
                    f = src[at]
                    after = src[jnp.minimum(at + 1, rows - 1)] if i == 7 else src[at + 1]
                    now = wy[at] * (f - after)
                    g = col_part(wx[at], f) + now - fy
                    fy = now
                    dst[at] = g
                    if low is None or low + i >= bound and high - i >= bound:
                        a = a + folded(f * f)
                    if low is None or low + i >= near_bound and high - i >= near_bound:
                        b = b + folded(f * g)
                return fy, a, b

            none = jnp.zeros((count, 128), F32)
            carry = (jnp.zeros((count, cols), F32), none, none)
            carry = tile(0, carry, 0, rows - 1)
            carry = lax.fori_loop(1, tiles - 1, lambda t, c: tile(t, c, None, None), carry)
            _, a, b = tile(tiles - 1, carry, rows - 8, 7)
            mom[first] = a
            mom[first + 1] = b

        apply_to(r, v, 0, 1, 2)
        apply_to(v, u, 2, 2, 3)

        def energy(t, carry, low, high):
            a, b = carry
            for i in range(8):
                if low is not None and (low + i < 3 or high - i < 3):
                    continue
                at = 8 * t + i
                f = u[at]
                d = f - next_col(f)
                e = wx[at] * d * d
                if low is None or high - i >= 4:
                    d = f - u[at + 1]
                    e = e + wy[at] * d * d
                a = a + folded(f * f)
                b = b + folded(e)
            return a, b

        none = jnp.zeros((count, 128), F32)
        carry = energy(0, (none, none), 0, rows - 1)
        carry = lax.fori_loop(1, tiles - 1, lambda t, c: energy(t, c, None, None), carry)
        mom[4], mom[5] = energy(tiles - 1, carry, rows - 8, 7)

    field = in_vmem(rows, count, cols)
    staged = pltpu.VMEM((blocks, count, rows + PAD, 128), F32)
    return pl.pallas_call(
        body,
        in_specs=[ANY] * 3,
        out_specs=[VMEM] * 7,
        out_shape=[field] * 5 + [in_vmem(3, count, cols), in_vmem(6, count, 128)],
        scratch_shapes=[staged] * 3 + [pltpu.SemaphoreType.DMA((2, 3, blocks))],
        name="interior",
        compiler_params=room(12),
    )(*(far_off(x) for x in (coh, gx, gy)))


def join(first, second, r, v, u, wx, wy, extra, mom):
    rows, count, cols = r.shape

    def body(got_first, got_second, r_in, v_in, u_in, wx_ref, wy_ref, ex, m_in, r_out, v_out, u_out, out):
        end = rows - 1
        even = lax.axis_index("strip") % 2 == 0
        ab = [jnp.where(even, got_second[i], got_first[i]) for i in range(5)]
        be = [jnp.where(even, got_first[i], got_second[i]) for i in range(6)]
        rr, vv, uu = ({}, {}, {})
        gx_w, gy_w = ({}, {})
        for i in (0, 1, 2, 3, end - 3, end - 2, end - 1, end):
            gx_w[i] = wx_ref[i]
            if i != end:
                gy_w[i] = wy_ref[i]
        gx_w[-1] = col_weights(ab[4])
        gy_w[-1] = ab[4] * ex[0]
        gy_w[-2] = ab[3] * ab[4]
        gy_w[end] = ex[1] * be[3]
        gy_w[end + 1] = be[3] * be[4]
        gy_w[end + 2] = be[4] * be[5]
        gx_w[end + 1] = col_weights(be[3])
        gx_w[end + 2] = col_weights(be[4])
        top = gy_w[-1] * ab[2]
        low = gy_w[end] * ex[2]
        rr[-2] = ab[0]
        rr[-1] = ab[1] - top
        rr[0] = r_in[0] + top
        rr[1], rr[2] = (r_in[1], r_in[2])
        rr[end - 2], rr[end - 1] = (r_in[end - 2], r_in[end - 1])
        rr[end] = r_in[end] - low
        rr[end + 1] = be[0] + low
        rr[end + 2] = be[1]
        rr[end + 3] = be[2]
        r_out[0] = rr[0]
        r_out[end] = rr[end]

        def applied(f, i):
            return (
                col_part(gx_w[i], f[i]) + gy_w[i] * (f[i] - f[i + 1]) - gy_w[i - 1] * (f[i - 1] - f[i])
            )

        sums = [m_in[j] for j in range(6)]

        def add(j, x):
            sums[j] = sums[j] + folded(x)

        for i in (-1, 0, 1, end - 1, end, end + 1, end + 2):
            vv[i] = applied(rr, i)
            if 0 <= i <= end:
                v_out[i] = vv[i]
        vv[2], vv[3] = (v_in[2], v_in[3])
        vv[end - 2], vv[end - 3] = (v_in[end - 2], v_in[end - 3])
        for i in (0, 1, 2, end - 2, end - 1, end, end + 1):
            uu[i] = applied(vv, i)
            if i <= end:
                u_out[i] = uu[i]
        uu[3], uu[end - 3] = (u_in[3], u_in[end - 3])
        for i in (0, end):
            add(0, rr[i] * rr[i])
        for i in (0, 1, end - 1, end):
            add(1, rr[i] * vv[i])
            add(2, vv[i] * vv[i])
        for i in (0, 1, 2, end - 2, end - 1, end):
            add(3, vv[i] * uu[i])
            add(4, uu[i] * uu[i])
            d = uu[i] - next_col(uu[i])
            h = uu[i] - uu[i + 1]
            add(5, gx_w[i] * d * d + gy_w[i] * h * h)
        h = uu[end - 3] - uu[end - 2]
        add(5, gy_w[end - 3] * h * h)
        lane = lax.broadcasted_iota(jnp.int32, (count, 128), 1)
        line = jnp.zeros((count, 128), F32)
        for j in range(6):
            line = jnp.where(lane == j, jnp.sum(sums[j], axis=1, keepdims=True), line)
        out[...] = line

    field = in_vmem(rows, count, cols)
    return pl.pallas_call(
        body,
        in_specs=[VMEM] * 9,
        out_specs=[VMEM] * 4,
        out_shape=[field] * 3 + [in_vmem(count, 128)],
        input_output_aliases={2: 0, 3: 1, 4: 2},
        name="join",
        compiler_params=room(4),
    )(near(first), near(second), r, v, u, wx, wy, extra, mom)


def strided_rows(ref, at, pitch, x):
    for b in range(ref.shape[0]):
        ref.at[b].reshape(x.shape[0] * pitch, 128)[pl.ds(at, x.shape[0], stride=pitch), :] = x[
            :, 128 * b : 128 * b + 128
        ]


def iterate(r, v, u, shares, groups, widths):
    rows, count, cols = r.shape
    high = rows // groups
    number = len(shares)

    def body(*refs):
        r_ref, v_ref, u_ref = refs[:3]
        terms = [ref[...] for ref in refs[3 : 3 + number]]
        out, keep, beside, *far = refs[3 + number :]
        while len(terms) > 1:
            terms = [sum(terms[i : i + 2][1:], terms[i]) for i in range(0, len(terms), 2)]
        m = terms[0]
        m0, m1, m2, m3, m4, m5 = (m[:, j : j + 1] for j in range(6))
        a00 = damping * m0 + m1
        a01 = damping * m1 + m2
        a02 = damping * m2 + m3
        a12 = damping * m3 + m4
        a22 = damping * m4 + m5

        def over(a, b, good):
            return jnp.where(good, a / jnp.where(good, b, 1.0), 0.0)

        ok0 = a00 > 0.0
        l10 = over(a01, a00, ok0)
        l20 = over(a02, a00, ok0)
        d1 = a02 - l10 * a01
        e12 = a12 - l10 * a02
        ok1 = d1 > TINY * a02
        l21 = over(e12, d1, ok1)
        d2 = a22 - l20 * a02 - l21 * e12
        ok2 = ok1 & (d2 > TINY * a22)
        y1 = m1 - l10 * m0
        y2 = m2 - l20 * m0 - l21 * y1
        c2 = over(y2, d2, ok2)
        c1 = over(y1, d1, ok1) - l21 * c2
        c0 = over(m0, a00, ok0) - l10 * c1 - l20 * c2
        lane = lax.broadcasted_iota(jnp.int32, (count, 128), 1)
        out[...] = jnp.where(lane == 0, c0, jnp.where(lane == 1, c1, c2))
        c0, c1, c2 = (jnp.broadcast_to(c, (count, cols)) for c in (c0, c1, c2))
        _, me = half_and_member(groups)

        def rows_for(mask, pieces):
            first = jnp.bitwise_xor(me, mask) * high
            for a in range(high):
                at = first + a
                x = c0 * r_ref[at] + c1 * v_ref[at] + c2 * u_ref[at]
                left = 0
                for piece in pieces:
                    wide = 128 * piece.shape[0]
                    strided_rows(piece, a, high, x[:, left : left + wide])
                    left += wide

        rows_for(0, [keep])
        rows_for(1, [beside])
        for mask in range(2, groups):
            rows_for(mask, [far[(mask - 2) * len(widths) + i] for i in range(len(widths))])

    return pl.pallas_call(
        body,
        in_specs=[VMEM] * (3 + number),
        out_specs=[VMEM] * (3 + (groups - 2) * len(widths)),
        out_shape=[in_vmem(count, 128)]
        + [in_vmem(cols // 128, count, high, 128)] * 2
        + [in_vmem(wide // 128, count, high, 128) for _ in range(groups - 2) for wide in widths],
        name="iterate",
        compiler_params=room(4),
    )(r, v, u, *(near(x) for x in shares))


def combine(r, v, u, weights):
    rows, count, cols = r.shape

    def body(r_ref, v_ref, u_ref, weights_ref, out, whole, sem):
        w = weights_ref[...]
        c0, c1, c2 = (jnp.broadcast_to(w[:, j : j + 1], (count, cols)) for j in range(3))

        def tile(t, _):
            for i in range(8):
                at = 8 * t + i
                strided_rows(whole, at, rows + PAD, c0 * r_ref[at] + c1 * v_ref[at] + c2 * u_ref[at])
            return 0

        lax.fori_loop(0, rows // 8, tile, 0)
        copies = [
            pltpu.make_async_copy(
                whole.at[b, :, pl.ds(0, rows), :], out.at[:, :, pl.ds(128 * b, 128)], sem.at[b]
            )
            for b in range(cols // 128)
        ]
        for copy in copies:
            copy.start()
        for copy in copies:
            copy.wait()

    return pl.pallas_call(
        body,
        in_specs=[VMEM] * 4,
        out_specs=ANY,
        out_shape=jax.ShapeDtypeStruct((count, rows, cols), F32),
        scratch_shapes=[
            pltpu.VMEM((cols // 128, count, rows + PAD, 128), F32),
            pltpu.SemaphoreType.DMA((cols // 128,)),
        ],
        name="combine",
        compiler_params=room(6),
    )(r, v, u, weights)


def half_sums(mapping, left, fields, start=None):
    groups = len(fields)
    blocks, count, high, _ = fields[-1].shape
    dates = DATES // 2
    share = dates // groups
    spots = [(b, a) for b in range(blocks) for a in range(0, high, 8)]

    def body(map_ref, *refs):
        us = refs[:groups]

        def sums_of(ds, accs):
            for m in range(groups):
                base = 0 if us[m].shape[0] == blocks else left // 128
                for k in range(count):
                    column = m * count + k
                    ws = [map_ref[d, column] for d in ds]
                    for i, (b, a) in enumerate(spots):
                        u = us[m][base + b, k, a : a + 8, :]
                        for acc, w in zip(accs, ws):
                            acc[i] = acc[i] + w * u
            return accs

        def store(out, d, acc):
            for (b, a), x in zip(spots, acc):
                out[b, d, a : a + 8, :] = x

        per = min(4 if len(spots) <= 2 else 2, share)

        def step_of(first, out, begin):
            def step(i, _):
                at = [per * i + j for j in range(per)]
                for d, acc in zip(at, sums_of([first + d for d in at], [begin(d) for d in at])):
                    store(out, d, acc)
                return 0

            return step

        if start is None:
            none = lambda d: [jnp.zeros((8, 128), F32) for _ in spots]
            lax.fori_loop(0, dates // per, step_of(0, refs[groups], none), 0)
        else:
            me = half_and_member(groups)[1]
            begun = refs[groups]
            for m, out in enumerate(refs[groups + 1 :]):
                first = jnp.bitwise_xor(me, m) * share
                begin = lambda d, first=first: [begun[b, first + d, a : a + 8, :] for b, a in spots]
                lax.fori_loop(0, share // per, step_of(dates + m * share, out, begin), 0)

    args = list(fields) + ([] if start is None else [start])
    out_shape = (
        [in_vmem(blocks, dates, high, 128)]
        if start is None
        else [in_vmem(blocks, share, high, 128)] * groups
    )
    return pl.pallas_call(
        body,
        in_specs=[SMEM] + [VMEM] * len(args),
        out_specs=[VMEM] * len(out_shape),
        out_shape=out_shape,
        name="cross_sums" if start is None else "own_sums",
        compiler_params=room(4),
    )(mapping, *(near(x) for x in args))


def assemble(parts, rows, cols):
    groups = len(parts[0])
    _, dates, high, _ = parts[0][0].shape
    flat = [x for chunk in parts for x in chunk]

    def body(*refs):
        _, me = half_and_member(groups)
        out = refs[-1]
        left = 0
        for i in range(len(parts)):
            blocks = parts[i][0].shape[0]
            for m in range(groups):
                first = pl.multiple_of(jnp.bitwise_xor(me, m) * high, 8)
                for b in range(blocks):
                    at = left + 128 * b
                    out[:, pl.ds(first, high), at : at + 128] = refs[i * groups + m][b]
            left += 128 * blocks

    return pl.pallas_call(
        body,
        in_specs=[VMEM] * len(flat),
        out_specs=VMEM,
        out_shape=jax.ShapeDtypeStruct((dates, rows, cols), F32),
        name="assemble",
        compiler_params=room(4),
    )(*(near(x) for x in flat))


def exchange(x, axis, mask):
    size = lax.axis_size(axis)
    return lax.ppermute(x, axis, [(i, i ^ mask) for i in range(size)])


def summands(x, axis):
    size, bit, terms = (lax.axis_size(axis), 1, [x])
    while bit < size:
        if len(terms) > 1:
            terms = [(terms[0] + terms[1]) + (terms[2] + terms[3])]
        masks = [bit, 2 * bit, 3 * bit] if 4 * bit <= size else [bit]
        terms = terms + [exchange(terms[0], axis, m) for m in masks]
        bit *= len(masks) + 1
    return terms


def on_device(grad_x, grad_y, coherence, pairs):
    strips, size = (lax.axis_size("strip"), lax.axis_size("ifg"))
    _, rows, cols = coherence.shape
    groups = size // 2
    widths = [cols * part // sum(SLICES) for part in SLICES]
    first, second = edges(coherence, grad_x, grad_y)
    first, second = (
        lax.ppermute(x, "strip", [p for i in range(at, strips - 1, 2) for p in ((i, i + 1), (i + 1, i))])
        for at, x in enumerate((first, second))
    )
    fields = interior(coherence, grad_x, grad_y)
    r, v, u, moments = join(first, second, *fields)
    shares = summands(moments, "strip")
    mapping = inverse_map(pairs, groups)
    weights, keep, beside, *far = iterate(r, v, u, shares, groups, widths)
    phase = combine(r, v, u, weights)
    beside = exchange(beside, "ifg", 1)
    parts, left = ([], 0)
    for i, wide in enumerate(widths):
        mine = [keep, beside]
        for m in range(2, groups):
            mine.append(exchange(far[(m - 2) * CHUNKS + i], "ifg", m))
        (other,) = half_sums(mapping, left, mine)
        other = exchange(other, "ifg", groups)
        full = half_sums(mapping, left, mine, other)
        part = [full[0]]
        for m in range(1, groups):
            part.append(exchange(full[m], "ifg", m))
        parts.append(part)
        left += wide
    return (phase, assemble(parts, rows, cols))


def solution(mesh):
    in_specs = (P("ifg", "strip", None), P("ifg", "strip", None), P("ifg", "strip", None), P())
    out_specs = (P("ifg", "strip", None), P("ifg", "strip", None))

    return jax.shard_map(on_device, mesh=mesh, in_specs=in_specs, out_specs=out_specs, check_vma=False)
```

```python
import jax
import jax.numpy as jnp
from jax import lax
from jax.experimental import pallas as pl
from jax.experimental.pallas import tpu as pltpu
from jax.sharding import PartitionSpec as P

DATES = 32
SLICES = (1, 2, 2, 2, 1)
CHUNKS = len(SLICES)
PAD = 8
EARLY = 12
damping = 0.1
TINY = 1e-6
F32 = jnp.float32
ANY = pl.BlockSpec(memory_space=pl.ANY)
SMEM = pl.BlockSpec(memory_space=pltpu.SMEM)
VMEM = pl.BlockSpec(memory_space=pltpu.VMEM)


def room(mib):
    return pltpu.CompilerParams(vmem_limit_bytes=mib * 2**20)


def near(x):
    return pltpu.with_memory_space_constraint(x, pltpu.VMEM)


def far_off(x):
    return pltpu.with_memory_space_constraint(x, pltpu.HBM)


def half_and_member(groups):
    index = lax.axis_index("ifg").astype(jnp.int32)
    return (index // groups, index % groups)


def in_vmem(*shape):
    return pltpu.VMEM(shape, F32)


def turned_cols(x, by, at):
    lane = lax.broadcasted_iota(jnp.int32, (x.shape[0], 128), 1)
    turned = [pltpu.roll(x[:, i : i + 128], by % 128, axis=1) for i in range(0, x.shape[1], 128)]
    moved = turned[-by:] + turned[:-by]
    return jnp.concatenate([jnp.where(lane == at, m, t) for m, t in zip(moved, turned)], axis=1)


def next_col(x):
    return turned_cols(x, -1, 127)


def prev_col(x):
    return turned_cols(x, 1, 0)


def col_weights(c):
    lane = lax.broadcasted_iota(jnp.int32, c.shape, 1)
    return jnp.where(lane < c.shape[1] - 1, c * next_col(c), 0.0)


def col_part(w, f):
    fx = w * (f - next_col(f))
    return fx - prev_col(fx)


def folded(x):
    parts = [x[:, i : i + 128] for i in range(0, x.shape[1], 128)]
    while len(parts) > 1:
        parts = [sum(parts[i : i + 2][1:], parts[i]) for i in range(0, len(parts), 2)]
    return parts[0]


def eliminated(w, pivots):
    row = lax.broadcasted_iota(jnp.int32, w.shape, 0)
    for j in pivots:
        pivot = w[j : j + 1] / w[j : j + 1, j : j + 1]
        w = jnp.where(row == j, pivot, w - w[:, j : j + 1] * pivot)
    return w


def inverse_map(pairs, groups):
    number = pairs.shape[0]
    inner = number // 2
    wide = -(-(DATES + number) // 128) * 128
    share = DATES // (2 * groups)
    count = number // (2 * groups)

    def body(pair, work):
        h, me = half_and_member(groups)

        def twin(i, each):
            return jnp.bitwise_xor(i // each, me) * each + i % each

        d = lax.broadcasted_iota(jnp.int32, (DATES, number), 0)
        half = DATES // 2
        slots = jnp.where(d < half, (1 - h) * half + d, h * half + twin(d % half, share))
        k = lax.broadcasted_iota(jnp.int32, (number, number), 1)
        source = jnp.where(k < inner, h * inner + twin(k % inner, count), (1 - h) * inner + k % inner)
        turn = (source == lax.broadcasted_iota(jnp.int32, (number, number), 0)).astype(F32)
        p = jnp.dot(
            pair[...].astype(F32), turn, precision=lax.Precision.HIGHEST, preferred_element_type=F32
        )
        slots = slots.astype(F32)
        back = (p[1:2] == slots).astype(F32) - (p[0:1] == slots).astype(F32)
        normal = 1.0 + lax.dot_general(
            back, back, (((1,), (1,)), ((), ())), precision=lax.Precision.HIGHEST, preferred_element_type=F32
        )
        work[...] = jnp.zeros_like(work)
        work[:, :DATES] = normal
        work[:, DATES : DATES + number] = back
        work[...] = eliminated(work[...], range(EARLY))

    return pl.pallas_call(
        body,
        in_specs=[VMEM],
        out_specs=VMEM,
        out_shape=in_vmem(DATES, wide),
        name="inverse_map",
        compiler_params=room(2),
    )(pairs.T)


def inverse_rest(work, inner):
    def body(begun, out, scratch):
        scratch[...] = eliminated(begun[...], range(EARLY, DATES))
        out[...] = scratch[:, DATES : DATES + inner]

    return pl.pallas_call(
        body,
        in_specs=[VMEM],
        out_specs=VMEM,
        out_shape=jax.ShapeDtypeStruct((DATES, inner), F32),
        scratch_shapes=[pltpu.VMEM(work.shape, F32)],
        name="inverse_rest",
        compiler_params=room(2),
    )(near(work))


def edges(coh, gx, gy):
    count, rows, cols = coh.shape
    last_tile = rows // 8 - 1

    def body(ct, xt, yt, cb, xb, yb, first, second):
        row = lax.broadcasted_iota(jnp.int32, (8, cols), 0)

        def partial_rhs(c, x, y):
            fx = col_weights(c) * x
            fy = jnp.where(row < 7, c * pltpu.roll(c, 7, axis=0) * y, 0.0)
            return -(fx - prev_col(fx) + fy - pltpu.roll(fy, 1, axis=0))

        def send(down, up):
            for k in range(count):
                c, y = (cb[k], yb[k])
                r = partial_rhs(c, xb[k], y)
                for i, x in enumerate((r[6:7], r[7:8], y[7:8], c[6:7], c[7:8])):
                    down[i, k : k + 1, :] = x
                c = ct[k]
                r = partial_rhs(c, xt[k], yt[k])
                for i in range(3):
                    up[i, k : k + 1, :] = r[i : i + 1]
                    up[3 + i, k : k + 1, :] = c[i : i + 1]
            down[5] = jnp.zeros((count, cols), F32)

        even = lax.axis_index("strip") % 2 == 0

        @pl.when(even)
        def _():
            send(first, second)

        @pl.when(jnp.logical_not(even))
        def _():
            send(second, first)

    top = pl.BlockSpec((count, 8, cols), lambda i: (0, 0, 0))
    bottom = pl.BlockSpec((count, 8, cols), lambda i: (0, last_tile, 0))
    return pl.pallas_call(
        body,
        grid=(1,),
        in_specs=[top, top, top, bottom, bottom, bottom],
        out_specs=[
            pl.BlockSpec((6, count, cols), lambda i: (0, 0, 0)),
            pl.BlockSpec((6, count, cols), lambda i: (0, 0, 0)),
        ],
        out_shape=[
            jax.ShapeDtypeStruct((6, count, cols), F32),
            jax.ShapeDtypeStruct((6, count, cols), F32),
        ],
        name="edges",
        compiler_params=room(8),
    )(*(far_off(x) for x in (coh, gx, gy, coh, gx, gy)))


def interior(coh, gx, gy):
    count, rows, cols = coh.shape
    tiles, blocks = (rows // 8, cols // 128)

    def body(c_hbm, x_hbm, y_hbm, r, v, u, wx, wy, extra, mom, cs, xs, ys, sems):
        half = rows // 2

        def copies(s):
            return [
                pltpu.make_async_copy(
                    src.at[:, pl.ds(s * half, half), pl.ds(128 * b, 128)],
                    dst.at[b, :, pl.ds(s * half, half), :],
                    sems.at[s, n, b],
                )
                for n, (src, dst) in enumerate(((c_hbm, cs), (x_hbm, xs), (y_hbm, ys)))
                for b in range(blocks)
            ]

        for s in range(2):
            for copy in copies(s):
                copy.start()

        def row_of(ref, i):
            return jnp.concatenate(
                [
                    ref.at[b].reshape(count * (rows + PAD), 128)[pl.ds(i, count, stride=rows + PAD), :]
                    for b in range(blocks)
                ],
                axis=1,
            )

        fy = jnp.zeros((count, cols), F32)
        for copy in copies(0):
            copy.wait()
        c = row_of(cs, 0)
        extra[0] = c
        for at in range(rows):
            if at == half - 1:
                for copy in copies(1):
                    copy.wait()
            w = col_weights(c)
            fx = w * row_of(xs, at)
            rhs = prev_col(fx) - fx + fy
            wx[at] = w
            if at < rows - 1:
                later = row_of(cs, at + 1)
                h = c * later
                wy[at] = h
                fy = h * row_of(ys, at)
                rhs = rhs - fy
                c = later
            else:
                wy[at] = jnp.zeros((count, cols), F32)
                extra[1] = c
                extra[2] = row_of(ys, at)
            r[at] = rhs

        def apply_to(src, dst, first, bound, near_bound):
            def tile(t, carry, low, high):
                fy, a, b = carry
                for i in range(8):
                    at = 8 * t + i
                    f = src[at]
                    after = src[jnp.minimum(at + 1, rows - 1)] if i == 7 else src[at + 1]
                    now = wy[at] * (f - after)
                    g = col_part(wx[at], f) + now - fy
                    fy = now
                    dst[at] = g
                    if low is None or low + i >= bound and high - i >= bound:
                        a = a + folded(f * f)
                    if low is None or low + i >= near_bound and high - i >= near_bound:
                        b = b + folded(f * g)
                return fy, a, b

            none = jnp.zeros((count, 128), F32)
            carry = (jnp.zeros((count, cols), F32), none, none)
            carry = tile(0, carry, 0, rows - 1)
            carry = lax.fori_loop(1, tiles - 1, lambda t, c: tile(t, c, None, None), carry)
            _, a, b = tile(tiles - 1, carry, rows - 8, 7)
            mom[first] = a
            mom[first + 1] = b

        apply_to(r, v, 0, 1, 2)
        apply_to(v, u, 2, 2, 3)

        def energy(t, carry, low, high):
            a, b = carry
            for i in range(8):
                if low is not None and (low + i < 3 or high - i < 3):
                    continue
                at = 8 * t + i
                f = u[at]
                d = f - next_col(f)
                e = wx[at] * d * d
                if low is None or high - i >= 4:
                    d = f - u[at + 1]
                    e = e + wy[at] * d * d
                a = a + folded(f * f)
                b = b + folded(e)
            return a, b

        none = jnp.zeros((count, 128), F32)
        carry = energy(0, (none, none), 0, rows - 1)
        carry = lax.fori_loop(1, tiles - 1, lambda t, c: energy(t, c, None, None), carry)
        mom[4], mom[5] = energy(tiles - 1, carry, rows - 8, 7)

    field = in_vmem(rows, count, cols)
    staged = pltpu.VMEM((blocks, count, rows + PAD, 128), F32)
    return pl.pallas_call(
        body,
        in_specs=[ANY] * 3,
        out_specs=[VMEM] * 7,
        out_shape=[field] * 5 + [in_vmem(3, count, cols), in_vmem(6, count, 128)],
        scratch_shapes=[staged] * 3 + [pltpu.SemaphoreType.DMA((2, 3, blocks))],
        name="interior",
        compiler_params=room(12),
    )(*(far_off(x) for x in (coh, gx, gy)))


def join(first, second, r, v, u, wx, wy, extra, mom):
    rows, count, cols = r.shape

    def body(got_first, got_second, r_in, v_in, u_in, wx_ref, wy_ref, ex, m_in, r_out, v_out, u_out, out):
        end = rows - 1
        even = lax.axis_index("strip") % 2 == 0
        ab = [jnp.where(even, got_second[i], got_first[i]) for i in range(5)]
        be = [jnp.where(even, got_first[i], got_second[i]) for i in range(6)]
        rr, vv, uu = ({}, {}, {})
        gx_w, gy_w = ({}, {})
        for i in (0, 1, 2, 3, end - 3, end - 2, end - 1, end):
            gx_w[i] = wx_ref[i]
            if i != end:
                gy_w[i] = wy_ref[i]
        gx_w[-1] = col_weights(ab[4])
        gy_w[-1] = ab[4] * ex[0]
        gy_w[-2] = ab[3] * ab[4]
        gy_w[end] = ex[1] * be[3]
        gy_w[end + 1] = be[3] * be[4]
        gy_w[end + 2] = be[4] * be[5]
        gx_w[end + 1] = col_weights(be[3])
        gx_w[end + 2] = col_weights(be[4])
        top = gy_w[-1] * ab[2]
        low = gy_w[end] * ex[2]
        rr[-2] = ab[0]
        rr[-1] = ab[1] - top
        rr[0] = r_in[0] + top
        rr[1], rr[2] = (r_in[1], r_in[2])
        rr[end - 2], rr[end - 1] = (r_in[end - 2], r_in[end - 1])
        rr[end] = r_in[end] - low
        rr[end + 1] = be[0] + low
        rr[end + 2] = be[1]
        rr[end + 3] = be[2]
        r_out[0] = rr[0]
        r_out[end] = rr[end]

        def applied(f, i):
            return (
                col_part(gx_w[i], f[i]) + gy_w[i] * (f[i] - f[i + 1]) - gy_w[i - 1] * (f[i - 1] - f[i])
            )

        sums = [m_in[j] for j in range(6)]

        def add(j, x):
            sums[j] = sums[j] + folded(x)

        for i in (-1, 0, 1, end - 1, end, end + 1, end + 2):
            vv[i] = applied(rr, i)
            if 0 <= i <= end:
                v_out[i] = vv[i]
        vv[2], vv[3] = (v_in[2], v_in[3])
        vv[end - 2], vv[end - 3] = (v_in[end - 2], v_in[end - 3])
        for i in (0, 1, 2, end - 2, end - 1, end, end + 1):
            uu[i] = applied(vv, i)
            if i <= end:
                u_out[i] = uu[i]
        uu[3], uu[end - 3] = (u_in[3], u_in[end - 3])
        for i in (0, end):
            add(0, rr[i] * rr[i])
        for i in (0, 1, end - 1, end):
            add(1, rr[i] * vv[i])
            add(2, vv[i] * vv[i])
        for i in (0, 1, 2, end - 2, end - 1, end):
            add(3, vv[i] * uu[i])
            add(4, uu[i] * uu[i])
            d = uu[i] - next_col(uu[i])
            h = uu[i] - uu[i + 1]
            add(5, gx_w[i] * d * d + gy_w[i] * h * h)
        h = uu[end - 3] - uu[end - 2]
        add(5, gy_w[end - 3] * h * h)
        lane = lax.broadcasted_iota(jnp.int32, (count, 128), 1)
        line = jnp.zeros((count, 128), F32)
        for j in range(6):
            line = jnp.where(lane == j, jnp.sum(sums[j], axis=1, keepdims=True), line)
        out[...] = line

    field = in_vmem(rows, count, cols)
    return pl.pallas_call(
        body,
        in_specs=[VMEM] * 9,
        out_specs=[VMEM] * 4,
        out_shape=[field] * 3 + [in_vmem(count, 128)],
        input_output_aliases={2: 0, 3: 1, 4: 2},
        name="join",
        compiler_params=room(4),
    )(near(first), near(second), r, v, u, wx, wy, extra, mom)


def strided_rows(ref, at, pitch, x):
    for b in range(ref.shape[0]):
        ref.at[b].reshape(x.shape[0] * pitch, 128)[pl.ds(at, x.shape[0], stride=pitch), :] = x[
            :, 128 * b : 128 * b + 128
        ]


def iterate(r, v, u, shares, groups, widths):
    rows, count, cols = r.shape
    high = rows // groups
    number = len(shares)

    def body(*refs):
        r_ref, v_ref, u_ref = refs[:3]
        terms = [ref[...] for ref in refs[3 : 3 + number]]
        out, keep, beside, *far = refs[3 + number :]
        while len(terms) > 1:
            terms = [sum(terms[i : i + 2][1:], terms[i]) for i in range(0, len(terms), 2)]
        m = terms[0]
        m0, m1, m2, m3, m4, m5 = (m[:, j : j + 1] for j in range(6))
        a00 = damping * m0 + m1
        a01 = damping * m1 + m2
        a02 = damping * m2 + m3
        a12 = damping * m3 + m4
        a22 = damping * m4 + m5

        def over(a, b, good):
            return jnp.where(good, a / jnp.where(good, b, 1.0), 0.0)

        ok0 = a00 > 0.0
        l10 = over(a01, a00, ok0)
        l20 = over(a02, a00, ok0)
        d1 = a02 - l10 * a01
        e12 = a12 - l10 * a02
        ok1 = d1 > TINY * a02
        l21 = over(e12, d1, ok1)
        d2 = a22 - l20 * a02 - l21 * e12
        ok2 = ok1 & (d2 > TINY * a22)
        y1 = m1 - l10 * m0
        y2 = m2 - l20 * m0 - l21 * y1
        c2 = over(y2, d2, ok2)
        c1 = over(y1, d1, ok1) - l21 * c2
        c0 = over(m0, a00, ok0) - l10 * c1 - l20 * c2
        lane = lax.broadcasted_iota(jnp.int32, (count, 128), 1)
        out[...] = jnp.where(lane == 0, c0, jnp.where(lane == 1, c1, c2))
        c0, c1, c2 = (jnp.broadcast_to(c, (count, cols)) for c in (c0, c1, c2))
        _, me = half_and_member(groups)

        def rows_for(mask, pieces):
            first = jnp.bitwise_xor(me, mask) * high
            for a in range(high):
                at = first + a
                x = c0 * r_ref[at] + c1 * v_ref[at] + c2 * u_ref[at]
                left = 0
                for piece in pieces:
                    wide = 128 * piece.shape[0]
                    strided_rows(piece, a, high, x[:, left : left + wide])
                    left += wide

        rows_for(0, [keep])
        rows_for(1, [beside])
        for mask in range(2, groups):
            rows_for(mask, [far[(mask - 2) * len(widths) + i] for i in range(len(widths))])

    return pl.pallas_call(
        body,
        in_specs=[VMEM] * (3 + number),
        out_specs=[VMEM] * (3 + (groups - 2) * len(widths)),
        out_shape=[in_vmem(count, 128)]
        + [in_vmem(cols // 128, count, high, 128)] * 2
        + [in_vmem(wide // 128, count, high, 128) for _ in range(groups - 2) for wide in widths],
        name="iterate",
        compiler_params=room(4),
    )(r, v, u, *(near(x) for x in shares))


def combine(r, v, u, weights):
    rows, count, cols = r.shape

    def body(r_ref, v_ref, u_ref, weights_ref, out, whole, sem):
        w = weights_ref[...]
        c0, c1, c2 = (jnp.broadcast_to(w[:, j : j + 1], (count, cols)) for j in range(3))

        def tile(t, _):
            for i in range(8):
                at = 8 * t + i
                strided_rows(whole, at, rows + PAD, c0 * r_ref[at] + c1 * v_ref[at] + c2 * u_ref[at])
            return 0

        lax.fori_loop(0, rows // 8, tile, 0)
        copies = [
            pltpu.make_async_copy(
                whole.at[b, :, pl.ds(0, rows), :], out.at[:, :, pl.ds(128 * b, 128)], sem.at[b]
            )
            for b in range(cols // 128)
        ]
        for copy in copies:
            copy.start()
        for copy in copies:
            copy.wait()

    return pl.pallas_call(
        body,
        in_specs=[VMEM] * 4,
        out_specs=ANY,
        out_shape=jax.ShapeDtypeStruct((count, rows, cols), F32),
        scratch_shapes=[
            pltpu.VMEM((cols // 128, count, rows + PAD, 128), F32),
            pltpu.SemaphoreType.DMA((cols // 128,)),
        ],
        name="combine",
        compiler_params=room(6),
    )(r, v, u, weights)


def half_sums(mapping, left, fields, start=None):
    groups = len(fields)
    blocks, count, high, _ = fields[-1].shape
    dates = DATES // 2
    share = dates // groups
    spots = [(b, a) for b in range(blocks) for a in range(0, high, 8)]

    def body(map_ref, *refs):
        us = refs[:groups]

        def sums_of(ds, accs):
            for m in range(groups):
                base = 0 if us[m].shape[0] == blocks else left // 128
                for k in range(count):
                    column = m * count + k
                    ws = [map_ref[d, column] for d in ds]
                    for i, (b, a) in enumerate(spots):
                        u = us[m][base + b, k, a : a + 8, :]
                        for acc, w in zip(accs, ws):
                            acc[i] = acc[i] + w * u
            return accs

        def store(out, d, acc):
            for (b, a), x in zip(spots, acc):
                out[b, d, a : a + 8, :] = x

        per = min(4 if len(spots) <= 2 else 2, share)

        def step_of(first, out, begin):
            def step(i, _):
                at = [per * i + j for j in range(per)]
                for d, acc in zip(at, sums_of([first + d for d in at], [begin(d) for d in at])):
                    store(out, d, acc)
                return 0

            return step

        if start is None:
            none = lambda d: [jnp.zeros((8, 128), F32) for _ in spots]
            lax.fori_loop(0, dates // per, step_of(0, refs[groups], none), 0)
        else:
            me = half_and_member(groups)[1]
            begun = refs[groups]
            for m, out in enumerate(refs[groups + 1 :]):
                first = jnp.bitwise_xor(me, m) * share
                begin = lambda d, first=first: [begun[b, first + d, a : a + 8, :] for b, a in spots]
                lax.fori_loop(0, share // per, step_of(dates + m * share, out, begin), 0)

    args = list(fields) + ([] if start is None else [start])
    out_shape = (
        [in_vmem(blocks, dates, high, 128)]
        if start is None
        else [in_vmem(blocks, share, high, 128)] * groups
    )
    return pl.pallas_call(
        body,
        in_specs=[SMEM] + [VMEM] * len(args),
        out_specs=[VMEM] * len(out_shape),
        out_shape=out_shape,
        name="cross_sums" if start is None else "own_sums",
        compiler_params=room(4),
    )(mapping, *(near(x) for x in args))


def assemble(parts, rows, cols):
    groups = len(parts[0])
    _, dates, high, _ = parts[0][0].shape
    flat = [x for chunk in parts for x in chunk]

    def body(*refs):
        _, me = half_and_member(groups)
        out = refs[-1]
        left = 0
        for i in range(len(parts)):
            blocks = parts[i][0].shape[0]
            for m in range(groups):
                first = pl.multiple_of(jnp.bitwise_xor(me, m) * high, 8)
                for b in range(blocks):
                    at = left + 128 * b
                    out[:, pl.ds(first, high), at : at + 128] = refs[i * groups + m][b]
            left += 128 * blocks

    return pl.pallas_call(
        body,
        in_specs=[VMEM] * len(flat),
        out_specs=VMEM,
        out_shape=jax.ShapeDtypeStruct((dates, rows, cols), F32),
        name="assemble",
        compiler_params=room(4),
    )(*(near(x) for x in flat))


def exchange(x, axis, mask):
    size = lax.axis_size(axis)
    return lax.ppermute(x, axis, [(i, i ^ mask) for i in range(size)])


def summands(x, axis):
    size, bit, terms = (lax.axis_size(axis), 1, [x])
    while bit < size:
        if len(terms) > 1:
            terms = [(terms[0] + terms[1]) + (terms[2] + terms[3])]
        masks = [bit, 2 * bit, 3 * bit] if 4 * bit <= size else [bit]
        terms = terms + [exchange(terms[0], axis, m) for m in masks]
        bit *= len(masks) + 1
    return terms


def on_device(grad_x, grad_y, coherence, pairs):
    strips, size = (lax.axis_size("strip"), lax.axis_size("ifg"))
    _, rows, cols = coherence.shape
    groups = size // 2
    widths = [cols * part // sum(SLICES) for part in SLICES]
    first, second = edges(coherence, grad_x, grad_y)
    first, second = (
        lax.ppermute(x, "strip", [p for i in range(at, strips - 1, 2) for p in ((i, i + 1), (i + 1, i))])
        for at, x in enumerate((first, second))
    )
    fields = interior(coherence, grad_x, grad_y)
    r, v, u, moments = join(first, second, *fields)
    shares = summands(moments, "strip")
    begun = inverse_map(pairs, groups)
    mapping = inverse_rest(begun, pairs.shape[0] // 2)
    weights, keep, beside, *far = iterate(r, v, u, shares, groups, widths)
    phase = combine(r, v, u, weights)
    beside = exchange(beside, "ifg", 1)
    parts, left = ([], 0)
    for i, wide in enumerate(widths):
        mine = [keep, beside]
        for m in range(2, groups):
            mine.append(exchange(far[(m - 2) * CHUNKS + i], "ifg", m))
        (other,) = half_sums(mapping, left, mine)
        other = exchange(other, "ifg", groups)
        full = half_sums(mapping, left, mine, other)
        part = [full[0]]
        for m in range(1, groups):
            part.append(exchange(full[m], "ifg", m))
        parts.append(part)
        left += wide
    return (phase, assemble(parts, rows, cols))


def solution(mesh):
    in_specs = (P("ifg", "strip", None), P("ifg", "strip", None), P("ifg", "strip", None), P())
    out_specs = (P("ifg", "strip", None), P("ifg", "strip", None))

    return jax.shard_map(on_device, mesh=mesh, in_specs=in_specs, out_specs=out_specs, check_vma=False)
```

```python
import jax
import jax.numpy as jnp
from jax import lax
from jax.experimental import pallas as pl
from jax.experimental.pallas import tpu as pltpu
from jax.sharding import PartitionSpec as P

DATES = 32
SLICES = (1, 2, 2, 2, 1)
CHUNKS = len(SLICES)
PAD = 8
EARLY = 18
damping = 0.1
TINY = 1e-6
F32 = jnp.float32
ANY = pl.BlockSpec(memory_space=pl.ANY)
SMEM = pl.BlockSpec(memory_space=pltpu.SMEM)
VMEM = pl.BlockSpec(memory_space=pltpu.VMEM)


def room(mib):
    return pltpu.CompilerParams(vmem_limit_bytes=mib * 2**20)


def near(x):
    return pltpu.with_memory_space_constraint(x, pltpu.VMEM)


def far_off(x):
    return pltpu.with_memory_space_constraint(x, pltpu.HBM)


def half_and_member(groups):
    index = lax.axis_index("ifg").astype(jnp.int32)
    return (index // groups, index % groups)


def in_vmem(*shape):
    return pltpu.VMEM(shape, F32)


def turned_cols(x, by, at):
    lane = lax.broadcasted_iota(jnp.int32, (x.shape[0], 128), 1)
    turned = [pltpu.roll(x[:, i : i + 128], by % 128, axis=1) for i in range(0, x.shape[1], 128)]
    moved = turned[-by:] + turned[:-by]
    return jnp.concatenate([jnp.where(lane == at, m, t) for m, t in zip(moved, turned)], axis=1)


def next_col(x):
    return turned_cols(x, -1, 127)


def prev_col(x):
    return turned_cols(x, 1, 0)


def col_weights(c):
    lane = lax.broadcasted_iota(jnp.int32, c.shape, 1)
    return jnp.where(lane < c.shape[1] - 1, c * next_col(c), 0.0)


def col_part(w, f):
    fx = w * (f - next_col(f))
    return fx - prev_col(fx)


def folded(x):
    parts = [x[:, i : i + 128] for i in range(0, x.shape[1], 128)]
    while len(parts) > 1:
        parts = [sum(parts[i : i + 2][1:], parts[i]) for i in range(0, len(parts), 2)]
    return parts[0]


def eliminated(w, pivots):
    row = lax.broadcasted_iota(jnp.int32, w.shape, 0)
    for j in pivots:
        pivot = w[j : j + 1] / w[j : j + 1, j : j + 1]
        w = jnp.where(row == j, pivot, w - w[:, j : j + 1] * pivot)
    return w


def inverse_map(pairs, groups):
    number = pairs.shape[0]
    inner = number // 2
    wide = -(-(DATES + number) // 128) * 128
    share = DATES // (2 * groups)
    count = number // (2 * groups)

    def body(pair, work):
        h, me = half_and_member(groups)

        def twin(i, each):
            return jnp.bitwise_xor(i // each, me) * each + i % each

        d = lax.broadcasted_iota(jnp.int32, (DATES, number), 0)
        half = DATES // 2
        slots = jnp.where(d < half, (1 - h) * half + d, h * half + twin(d % half, share))
        k = lax.broadcasted_iota(jnp.int32, (number, number), 1)
        source = jnp.where(k < inner, h * inner + twin(k % inner, count), (1 - h) * inner + k % inner)
        turn = (source == lax.broadcasted_iota(jnp.int32, (number, number), 0)).astype(F32)
        p = jnp.dot(
            pair[...].astype(F32), turn, precision=lax.Precision.HIGHEST, preferred_element_type=F32
        )
        slots = slots.astype(F32)
        back = (p[1:2] == slots).astype(F32) - (p[0:1] == slots).astype(F32)
        normal = 1.0 + lax.dot_general(
            back, back, (((1,), (1,)), ((), ())), precision=lax.Precision.HIGHEST, preferred_element_type=F32
        )
        work[...] = jnp.zeros_like(work)
        work[:, :DATES] = normal
        work[:, DATES : DATES + number] = back
        work[...] = eliminated(work[...], range(EARLY))

    return pl.pallas_call(
        body,
        in_specs=[VMEM],
        out_specs=VMEM,
        out_shape=in_vmem(DATES, wide),
        name="inverse_map",
        compiler_params=room(2),
    )(pairs.T)


def inverse_rest(work, inner):
    def body(begun, out, scratch):
        scratch[...] = eliminated(begun[...], range(EARLY, DATES))
        out[...] = scratch[:, DATES : DATES + inner]

    return pl.pallas_call(
        body,
        in_specs=[VMEM],
        out_specs=VMEM,
        out_shape=jax.ShapeDtypeStruct((DATES, inner), F32),
        scratch_shapes=[pltpu.VMEM(work.shape, F32)],
        name="inverse_rest",
        compiler_params=room(2),
    )(near(work))


def edges(coh, gx, gy):
    count, rows, cols = coh.shape
    last_tile = rows // 8 - 1

    def body(ct, xt, yt, cb, xb, yb, first, second):
        row = lax.broadcasted_iota(jnp.int32, (8, cols), 0)

        def partial_rhs(c, x, y):
            fx = col_weights(c) * x
            fy = jnp.where(row < 7, c * pltpu.roll(c, 7, axis=0) * y, 0.0)
            return -(fx - prev_col(fx) + fy - pltpu.roll(fy, 1, axis=0))

        def send(down, up):
            for k in range(count):
                c, x, y = (jnp.where(row < 4, t[k], b[k]) for t, b in ((ct, cb), (xt, xb), (yt, yb)))
                r = partial_rhs(c, x, y)
                for i, x in enumerate((r[6:7], r[7:8], y[7:8], c[6:7], c[7:8])):
                    down[i, k : k + 1, :] = x
                for i in range(3):
                    up[i, k : k + 1, :] = r[i : i + 1]
                    up[3 + i, k : k + 1, :] = c[i : i + 1]
            down[5] = jnp.zeros((count, cols), F32)

        even = lax.axis_index("strip") % 2 == 0

        @pl.when(even)
        def _():
            send(first, second)

        @pl.when(jnp.logical_not(even))
        def _():
            send(second, first)

    top = pl.BlockSpec((count, 8, cols), lambda i: (0, 0, 0))
    bottom = pl.BlockSpec((count, 8, cols), lambda i: (0, last_tile, 0))
    return pl.pallas_call(
        body,
        grid=(1,),
        in_specs=[top, top, top, bottom, bottom, bottom],
        out_specs=[
            pl.BlockSpec((6, count, cols), lambda i: (0, 0, 0)),
            pl.BlockSpec((6, count, cols), lambda i: (0, 0, 0)),
        ],
        out_shape=[
            jax.ShapeDtypeStruct((6, count, cols), F32),
            jax.ShapeDtypeStruct((6, count, cols), F32),
        ],
        name="edges",
        compiler_params=room(8),
    )(*(far_off(x) for x in (coh, gx, gy, coh, gx, gy)))


def interior(coh, gx, gy):
    count, rows, cols = coh.shape
    tiles, blocks = (rows // 8, cols // 128)

    def body(c_hbm, x_hbm, y_hbm, r, v, u, wx, wy, extra, mom, cs, xs, ys, sems):
        half = rows // 2

        def copies(s):
            return [
                pltpu.make_async_copy(
                    src.at[:, pl.ds(s * half, half), pl.ds(128 * b, 128)],
                    dst.at[b, :, pl.ds(s * half, half), :],
                    sems.at[s, n, b],
                )
                for n, (src, dst) in enumerate(((c_hbm, cs), (x_hbm, xs), (y_hbm, ys)))
                for b in range(blocks)
            ]

        for s in range(2):
            for copy in copies(s):
                copy.start()

        def row_of(ref, i):
            return jnp.concatenate(
                [
                    ref.at[b].reshape(count * (rows + PAD), 128)[pl.ds(i, count, stride=rows + PAD), :]
                    for b in range(blocks)
                ],
                axis=1,
            )

        fy = jnp.zeros((count, cols), F32)
        for copy in copies(0):
            copy.wait()
        c = row_of(cs, 0)
        extra[0] = c
        for at in range(rows):
            if at == half - 1:
                for copy in copies(1):
                    copy.wait()
            w = col_weights(c)
            fx = w * row_of(xs, at)
            rhs = prev_col(fx) - fx + fy
            wx[at] = w
            if at < rows - 1:
                later = row_of(cs, at + 1)
                h = c * later
                wy[at] = h
                fy = h * row_of(ys, at)
                rhs = rhs - fy
                c = later
            else:
                wy[at] = jnp.zeros((count, cols), F32)
                extra[1] = c
                extra[2] = row_of(ys, at)
            r[at] = rhs

        def apply_to(src, dst, first, bound, near_bound):
            def tile(t, carry, low, high):
                fy, a, b = carry
                for i in range(8):
                    at = 8 * t + i
                    f = src[at]
                    after = src[jnp.minimum(at + 1, rows - 1)] if i == 7 else src[at + 1]
                    now = wy[at] * (f - after)
                    g = col_part(wx[at], f) + now - fy
                    fy = now
                    dst[at] = g
                    if low is None or low + i >= bound and high - i >= bound:
                        a = a + folded(f * f)
                    if low is None or low + i >= near_bound and high - i >= near_bound:
                        b = b + folded(f * g)
                return fy, a, b

            none = jnp.zeros((count, 128), F32)
            carry = (jnp.zeros((count, cols), F32), none, none)
            carry = tile(0, carry, 0, rows - 1)
            carry = lax.fori_loop(1, tiles - 1, lambda t, c: tile(t, c, None, None), carry)
            _, a, b = tile(tiles - 1, carry, rows - 8, 7)
            mom[first] = a
            mom[first + 1] = b

        apply_to(r, v, 0, 1, 2)
        apply_to(v, u, 2, 2, 3)

        def energy(t, carry, low, high):
            a, b = carry
            for i in range(8):
                if low is not None and (low + i < 3 or high - i < 3):
                    continue
                at = 8 * t + i
                f = u[at]
                d = f - next_col(f)
                e = wx[at] * d * d
                if low is None or high - i >= 4:
                    d = f - u[at + 1]
                    e = e + wy[at] * d * d
                a = a + folded(f * f)
                b = b + folded(e)
            return a, b

        none = jnp.zeros((count, 128), F32)
        carry = energy(0, (none, none), 0, rows - 1)
        carry = lax.fori_loop(1, tiles - 1, lambda t, c: energy(t, c, None, None), carry)
        mom[4], mom[5] = energy(tiles - 1, carry, rows - 8, 7)

    field = in_vmem(rows, count, cols)
    staged = pltpu.VMEM((blocks, count, rows + PAD, 128), F32)
    return pl.pallas_call(
        body,
        in_specs=[ANY] * 3,
        out_specs=[VMEM] * 7,
        out_shape=[field] * 5 + [in_vmem(3, count, cols), in_vmem(6, count, 128)],
        scratch_shapes=[staged] * 3 + [pltpu.SemaphoreType.DMA((2, 3, blocks))],
        name="interior",
        compiler_params=room(12),
    )(*(far_off(x) for x in (coh, gx, gy)))


def join(first, second, r, v, u, wx, wy, extra, mom):
    rows, count, cols = r.shape

    def body(got_first, got_second, r_in, v_in, u_in, wx_ref, wy_ref, ex, m_in, r_out, v_out, u_out, out):
        end = rows - 1
        even = lax.axis_index("strip") % 2 == 0
        ab = [jnp.where(even, got_second[i], got_first[i]) for i in range(5)]
        be = [jnp.where(even, got_first[i], got_second[i]) for i in range(6)]
        rr, vv, uu = ({}, {}, {})
        gx_w, gy_w = ({}, {})
        for i in (0, 1, 2, 3, end - 3, end - 2, end - 1, end):
            gx_w[i] = wx_ref[i]
            if i != end:
                gy_w[i] = wy_ref[i]
        gx_w[-1] = col_weights(ab[4])
        gy_w[-1] = ab[4] * ex[0]
        gy_w[-2] = ab[3] * ab[4]
        gy_w[end] = ex[1] * be[3]
        gy_w[end + 1] = be[3] * be[4]
        gy_w[end + 2] = be[4] * be[5]
        gx_w[end + 1] = col_weights(be[3])
        gx_w[end + 2] = col_weights(be[4])
        top = gy_w[-1] * ab[2]
        low = gy_w[end] * ex[2]
        rr[-2] = ab[0]
        rr[-1] = ab[1] - top
        rr[0] = r_in[0] + top
        rr[1], rr[2] = (r_in[1], r_in[2])
        rr[end - 2], rr[end - 1] = (r_in[end - 2], r_in[end - 1])
        rr[end] = r_in[end] - low
        rr[end + 1] = be[0] + low
        rr[end + 2] = be[1]
        rr[end + 3] = be[2]
        r_out[0] = rr[0]
        r_out[end] = rr[end]

        def applied(f, i):
            return (
                col_part(gx_w[i], f[i]) + gy_w[i] * (f[i] - f[i + 1]) - gy_w[i - 1] * (f[i - 1] - f[i])
            )

        sums = [m_in[j] for j in range(6)]

        def add(j, x):
            sums[j] = sums[j] + folded(x)

        for i in (-1, 0, 1, end - 1, end, end + 1, end + 2):
            vv[i] = applied(rr, i)
            if 0 <= i <= end:
                v_out[i] = vv[i]
        vv[2], vv[3] = (v_in[2], v_in[3])
        vv[end - 2], vv[end - 3] = (v_in[end - 2], v_in[end - 3])
        for i in (0, 1, 2, end - 2, end - 1, end, end + 1):
            uu[i] = applied(vv, i)
            if i <= end:
                u_out[i] = uu[i]
        uu[3], uu[end - 3] = (u_in[3], u_in[end - 3])
        for i in (0, end):
            add(0, rr[i] * rr[i])
        for i in (0, 1, end - 1, end):
            add(1, rr[i] * vv[i])
            add(2, vv[i] * vv[i])
        for i in (0, 1, 2, end - 2, end - 1, end):
            add(3, vv[i] * uu[i])
            add(4, uu[i] * uu[i])
            d = uu[i] - next_col(uu[i])
            h = uu[i] - uu[i + 1]
            add(5, gx_w[i] * d * d + gy_w[i] * h * h)
        h = uu[end - 3] - uu[end - 2]
        add(5, gy_w[end - 3] * h * h)
        lane = lax.broadcasted_iota(jnp.int32, (count, 128), 1)
        line = jnp.zeros((count, 128), F32)
        for j in range(6):
            line = jnp.where(lane == j, jnp.sum(sums[j], axis=1, keepdims=True), line)
        out[...] = line

    field = in_vmem(rows, count, cols)
    return pl.pallas_call(
        body,
        in_specs=[VMEM] * 9,
        out_specs=[VMEM] * 4,
        out_shape=[field] * 3 + [in_vmem(count, 128)],
        input_output_aliases={2: 0, 3: 1, 4: 2},
        name="join",
        compiler_params=room(4),
    )(near(first), near(second), r, v, u, wx, wy, extra, mom)


def strided_rows(ref, at, pitch, x):
    for b in range(ref.shape[0]):
        ref.at[b].reshape(x.shape[0] * pitch, 128)[pl.ds(at, x.shape[0], stride=pitch), :] = x[
            :, 128 * b : 128 * b + 128
        ]


def iterate(r, v, u, shares, groups, widths):
    rows, count, cols = r.shape
    high = rows // groups
    number = len(shares)

    def body(*refs):
        r_ref, v_ref, u_ref = refs[:3]
        terms = [ref[...] for ref in refs[3 : 3 + number]]
        out, keep, beside, *far = refs[3 + number :]
        while len(terms) > 1:
            terms = [sum(terms[i : i + 2][1:], terms[i]) for i in range(0, len(terms), 2)]
        m = terms[0]
        m0, m1, m2, m3, m4, m5 = (m[:, j : j + 1] for j in range(6))
        a00 = damping * m0 + m1
        a01 = damping * m1 + m2
        a02 = damping * m2 + m3
        a12 = damping * m3 + m4
        a22 = damping * m4 + m5

        def over(a, b, good):
            return jnp.where(good, a / jnp.where(good, b, 1.0), 0.0)

        ok0 = a00 > 0.0
        l10 = over(a01, a00, ok0)
        l20 = over(a02, a00, ok0)
        d1 = a02 - l10 * a01
        e12 = a12 - l10 * a02
        ok1 = d1 > TINY * a02
        l21 = over(e12, d1, ok1)
        d2 = a22 - l20 * a02 - l21 * e12
        ok2 = ok1 & (d2 > TINY * a22)
        y1 = m1 - l10 * m0
        y2 = m2 - l20 * m0 - l21 * y1
        c2 = over(y2, d2, ok2)
        c1 = over(y1, d1, ok1) - l21 * c2
        c0 = over(m0, a00, ok0) - l10 * c1 - l20 * c2
        lane = lax.broadcasted_iota(jnp.int32, (count, 128), 1)
        out[...] = jnp.where(lane == 0, c0, jnp.where(lane == 1, c1, c2))
        c0, c1, c2 = (jnp.broadcast_to(c, (count, cols)) for c in (c0, c1, c2))
        _, me = half_and_member(groups)

        def rows_for(mask, pieces):
            first = jnp.bitwise_xor(me, mask) * high
            for a in range(high):
                at = first + a
                x = c0 * r_ref[at] + c1 * v_ref[at] + c2 * u_ref[at]
                left = 0
                for piece in pieces:
                    wide = 128 * piece.shape[0]
                    strided_rows(piece, a, high, x[:, left : left + wide])
                    left += wide

        rows_for(0, [keep])
        rows_for(1, [beside])
        for mask in range(2, groups):
            rows_for(mask, [far[(mask - 2) * len(widths) + i] for i in range(len(widths))])

    return pl.pallas_call(
        body,
        in_specs=[VMEM] * (3 + number),
        out_specs=[VMEM] * (3 + (groups - 2) * len(widths)),
        out_shape=[in_vmem(count, 128)]
        + [in_vmem(cols // 128, count, high, 128)] * 2
        + [in_vmem(wide // 128, count, high, 128) for _ in range(groups - 2) for wide in widths],
        name="iterate",
        compiler_params=room(4),
    )(r, v, u, *(near(x) for x in shares))


def combine(r, v, u, weights):
    rows, count, cols = r.shape

    def body(r_ref, v_ref, u_ref, weights_ref, out, whole, sem):
        w = weights_ref[...]
        c0, c1, c2 = (jnp.broadcast_to(w[:, j : j + 1], (count, cols)) for j in range(3))

        def tile(t, _):
            for i in range(8):
                at = 8 * t + i
                strided_rows(whole, at, rows + PAD, c0 * r_ref[at] + c1 * v_ref[at] + c2 * u_ref[at])
            return 0

        lax.fori_loop(0, rows // 8, tile, 0)
        copies = [
            pltpu.make_async_copy(
                whole.at[b, :, pl.ds(0, rows), :], out.at[:, :, pl.ds(128 * b, 128)], sem.at[b]
            )
            for b in range(cols // 128)
        ]
        for copy in copies:
            copy.start()
        for copy in copies:
            copy.wait()

    return pl.pallas_call(
        body,
        in_specs=[VMEM] * 4,
        out_specs=ANY,
        out_shape=jax.ShapeDtypeStruct((count, rows, cols), F32),
        scratch_shapes=[
            pltpu.VMEM((cols // 128, count, rows + PAD, 128), F32),
            pltpu.SemaphoreType.DMA((cols // 128,)),
        ],
        name="combine",
        compiler_params=room(6),
    )(r, v, u, weights)


def half_sums(mapping, left, fields, start=None):
    groups = len(fields)
    blocks, count, high, _ = fields[-1].shape
    dates = DATES // 2
    share = dates // groups
    spots = [(b, a) for b in range(blocks) for a in range(0, high, 8)]

    def body(map_ref, *refs):
        us = refs[:groups]

        def sums_of(ds, accs):
            for m in range(groups):
                base = 0 if us[m].shape[0] == blocks else left // 128
                for k in range(count):
                    column = m * count + k
                    ws = [map_ref[d, column] for d in ds]
                    for i, (b, a) in enumerate(spots):
                        u = us[m][base + b, k, a : a + 8, :]
                        for acc, w in zip(accs, ws):
                            acc[i] = acc[i] + w * u
            return accs

        def store(out, d, acc):
            for (b, a), x in zip(spots, acc):
                out[b, d, a : a + 8, :] = x

        per = min(4, share)

        def step_of(first, out, begin):
            def step(i, _):
                at = [per * i + j for j in range(per)]
                for d, acc in zip(at, sums_of([first + d for d in at], [begin(d) for d in at])):
                    store(out, d, acc)
                return 0

            return step

        if start is None:
            none = lambda d: [jnp.zeros((8, 128), F32) for _ in spots]
            lax.fori_loop(0, dates // per, step_of(0, refs[groups], none), 0)
        else:
            me = half_and_member(groups)[1]
            begun = refs[groups]
            for m, out in enumerate(refs[groups + 1 :]):
                first = jnp.bitwise_xor(me, m) * share
                begin = lambda d, first=first: [begun[b, first + d, a : a + 8, :] for b, a in spots]
                lax.fori_loop(0, share // per, step_of(dates + m * share, out, begin), 0)

    args = list(fields) + ([] if start is None else [start])
    out_shape = (
        [in_vmem(blocks, dates, high, 128)]
        if start is None
        else [in_vmem(blocks, share, high, 128)] * groups
    )
    return pl.pallas_call(
        body,
        in_specs=[SMEM] + [VMEM] * len(args),
        out_specs=[VMEM] * len(out_shape),
        out_shape=out_shape,
        name="cross_sums" if start is None else "own_sums",
        compiler_params=room(4),
    )(mapping, *(near(x) for x in args))


def assemble(parts, rows, cols):
    groups = len(parts[0])
    _, dates, high, _ = parts[0][0].shape
    flat = [x for chunk in parts for x in chunk]

    def body(*refs):
        _, me = half_and_member(groups)
        out = refs[-1]
        left = 0
        for i in range(len(parts)):
            blocks = parts[i][0].shape[0]
            for m in range(groups):
                first = pl.multiple_of(jnp.bitwise_xor(me, m) * high, 8)
                for b in range(blocks):
                    at = left + 128 * b
                    out[:, pl.ds(first, high), at : at + 128] = refs[i * groups + m][b]
            left += 128 * blocks

    return pl.pallas_call(
        body,
        in_specs=[VMEM] * len(flat),
        out_specs=VMEM,
        out_shape=jax.ShapeDtypeStruct((dates, rows, cols), F32),
        name="assemble",
        compiler_params=room(4),
    )(*(near(x) for x in flat))


def exchange(x, axis, mask):
    size = lax.axis_size(axis)
    return lax.ppermute(x, axis, [(i, i ^ mask) for i in range(size)])


def summands(x, axis):
    size, bit, terms = (lax.axis_size(axis), 1, [x])
    while bit < size:
        if len(terms) > 1:
            terms = [(terms[0] + terms[1]) + (terms[2] + terms[3])]
        masks = [bit, 2 * bit, 3 * bit] if 4 * bit <= size else [bit]
        terms = terms + [exchange(terms[0], axis, m) for m in masks]
        bit *= len(masks) + 1
    return terms


def on_device(grad_x, grad_y, coherence, pairs):
    strips, size = (lax.axis_size("strip"), lax.axis_size("ifg"))
    _, rows, cols = coherence.shape
    groups = size // 2
    widths = [cols * part // sum(SLICES) for part in SLICES]
    first, second = edges(coherence, grad_x, grad_y)
    first, second = (
        lax.ppermute(x, "strip", [p for i in range(at, strips - 1, 2) for p in ((i, i + 1), (i + 1, i))])
        for at, x in enumerate((first, second))
    )
    fields = interior(coherence, grad_x, grad_y)
    r, v, u, moments = join(first, second, *fields)
    shares = summands(moments, "strip")
    begun = inverse_map(pairs, groups)
    mapping = inverse_rest(begun, pairs.shape[0] // 2)
    weights, keep, beside, *far = iterate(r, v, u, shares, groups, widths)
    phase = combine(r, v, u, weights)
    beside = exchange(beside, "ifg", 1)
    parts, left = ([], 0)
    for i, wide in enumerate(widths):
        mine = [keep, beside]
        for m in range(2, groups):
            mine.append(exchange(far[(m - 2) * CHUNKS + i], "ifg", m))
        (other,) = half_sums(mapping, left, mine)
        other = exchange(other, "ifg", groups)
        full = half_sums(mapping, left, mine, other)
        part = [full[0]]
        for m in range(1, groups):
            part.append(exchange(full[m], "ifg", m))
        parts.append(part)
        left += wide
    return (phase, assemble(parts, rows, cols))


def solution(mesh):
    in_specs = (P("ifg", "strip", None), P("ifg", "strip", None), P("ifg", "strip", None), P())
    out_specs = (P("ifg", "strip", None), P("ifg", "strip", None))

    return jax.shard_map(on_device, mesh=mesh, in_specs=in_specs, out_specs=out_specs, check_vma=False)
```
